256 devices in a mesh: blk: 64 (over y, z, core), band: 4 (over x).
Axes of the slice: x: 4, y: 4, z: 8, core: 2. Of those that a mesh axis runs over, the one named last changes fastest.
Arguments:
- grid_nodes: bfloat16 [131072, 512], P(('blk', 'band')), may hold values from -6 to 6
- enc_edges: bfloat16 [262144, 512], P(('blk', 'band')), may hold values from -6 to 6
- enc_sender: int32 [262144], P(('blk', 'band')), may hold values from 0 to 511, as said below
- enc_slot: int32 [262144], P(('blk', 'band')), may hold values from 0 to 511
- enc_slot_node: int32 [256, 512], P(('blk', 'band')), may hold values from 0 to 639
- mesh_nodes: bfloat16 [40960, 512], P('blk'), may hold values from -6 to 6
- mesh_edges: bfloat16 [262144, 512], P(('blk', 'band')), may hold values from -6 to 6
- mesh_sender: int32 [262144], P(('blk', 'band')), may hold values from 0 to 511
- mesh_receiver: int32 [262144], P(('blk', 'band')), may hold values from 0 to 639
- mesh_send_node: int32 [256, 512], P(('blk', 'band')), may hold values from 0 to 639
- grid_weights: bfloat16 [2, 512, 512], replicated, may hold values from -0.25 to 0.25
- enc_edge_weights: bfloat16 [4, 512, 512], replicated, may hold values from -0.25 to 0.25
- enc_node_weights: bfloat16 [3, 512, 512], replicated, may hold values from -0.25 to 0.25
- proc_edge_weights: bfloat16 [4, 512, 512], replicated, may hold values from -0.25 to 0.25
- proc_node_weights: bfloat16 [3, 512, 512], replicated, may hold values from -0.25 to 0.25
- biases: float32 [5, 2, 512], replicated, may hold values from -3 to 3
- gains: float32 [5, 512], replicated, may hold values from 0.5 to 1.5
Outputs:
- grid_out: bfloat16 [131072, 512], P(('blk', 'band'))
- mesh_out: bfloat16 [40960, 512], P(('blk', 'band'))
The draws below stay inside these ranges and needn't reach their ends.
Inputs may be any that keep to these rules, and one draw needn't show every extreme that they name: `enc_sender`: within each device's 1024 edges the values never fall, and every one of the device's 512 grid rows is a sender.
All inputs are finite; a program needn't handle non-finite values.
Results may differ from the reference program's by a relative error of at most 0.014.
Values may be sent and summed in bfloat16 or wider, within the bound.
A program may use at most 64 MiB of HBM per device.

```python
import jax
import jax.numpy as jnp
from jax import lax

D = 512
GRID_DEV = 512
MESH_P = 640
MEDGE_DEV = 1024
NEIGH = 8
CAP = 64
MCAP = 8
EDGE_DEV = 1024
GRID = 131072
EDGES = 262144
MESH = 40960
MEDGES = 262144
N_BLK = 64
N_BAND = 4


def draw_enc_sender(key, part):
    devices = EDGES // EDGE_DEV
    extra_rows = jax.random.randint(key, (devices, EDGE_DEV - GRID_DEV), 0, GRID_DEV, dtype=jnp.int32)
    each_node = jnp.broadcast_to(jnp.arange(GRID_DEV, dtype=jnp.int32), (devices, GRID_DEV))
    return jnp.sort(jnp.concatenate([each_node, extra_rows], axis=1), axis=1).reshape(EDGES)


def draw_mesh_sender(key, part):
    key_near, key_offset, key_far, key_slot = jax.random.split(jax.random.fold_in(key, 17), 4)
    blk_index = jnp.arange(MEDGES, dtype=jnp.int32) // MEDGE_DEV // N_BAND
    nearby = jax.random.randint(key_near, (MEDGES,), 0, 4, dtype=jnp.int32) < 3
    offset = jax.random.randint(key_offset, (MEDGES,), 0, NEIGH, dtype=jnp.int32) - NEIGH // 2
    distant = jax.random.randint(key_far, (MEDGES,), 0, N_BLK, dtype=jnp.int32)
    patch = jnp.where(nearby, (blk_index + offset) % N_BLK, distant)
    slot = jax.random.randint(key_slot, (MEDGES,), 0, MCAP, dtype=jnp.int32)
    return (patch * MCAP + slot).astype(jnp.int32)


def place_ends(array, own_key, low, high):
    dims = array.shape
    spot = [jax.random.randint(jax.random.fold_in(own_key, axis), (), 0, dims[axis]) for axis in range(len(dims))]
    array = array.at[tuple(spot)].set(low)
    longest = dims.index(max(dims))
    spot[longest] = (spot[longest] + 1) % dims[longest]
    return array.at[tuple(spot)].set(high)


def block_scale(own_key, shape, cuts, least, largest):
    loudness, own = 1.0, jax.random.fold_in(own_key, 6)
    for dim, shards_of in cuts:
        heights = jnp.exp(jax.random.uniform(jax.random.fold_in(own, dim), (shards_of,), jnp.float32, least / len(cuts), largest / len(cuts)))
        loudness = loudness * jnp.repeat(heights, shape[dim] // shards_of).reshape([-1 if axis == dim else 1 for axis in range(len(shape))])
    return loudness


def scatter_about(rng, extent, scale, bound, shards=(), kind=jnp.bfloat16):
    result = scale * jax.random.normal(rng, extent, jnp.float32)
    if shards:
        result = result * block_scale(rng, extent, shards, -0.22, 0.18)
    return jnp.clip(result, -bound, bound).astype(kind)


def setup_inputs(seed: int = 0) -> dict:
    arg_keys = jax.random.split(jax.random.key(seed), 18)
    grid_nodes = scatter_about(arg_keys[0], (GRID, D), 1.0, 6.0, ((0, 256),))
    enc_edges = scatter_about(arg_keys[1], (EDGES, D), 1.0, 6.0, ((0, 256),))
    enc_sender = draw_enc_sender(jax.random.fold_in(arg_keys[17], 71), 0)
    enc_slot = place_ends(jax.random.randint(arg_keys[3], (EDGES,), 0, NEIGH * CAP), jax.random.fold_in(arg_keys[3], 1), 0, (NEIGH * CAP) - 1).astype(jnp.int32)
    enc_slot_node = place_ends(jax.random.randint(arg_keys[4], (N_BLK * N_BAND, NEIGH * CAP), 0, MESH_P), jax.random.fold_in(arg_keys[4], 1), 0, MESH_P - 1).astype(jnp.int32)
    mesh_nodes = scatter_about(arg_keys[5], (MESH, D), 1.0, 6.0, ((0, 64),))
    mesh_edges = scatter_about(arg_keys[6], (MEDGES, D), 1.0, 6.0, ((0, 256),))
    mesh_sender = draw_mesh_sender(jax.random.fold_in(arg_keys[17], 71), 0)
    mesh_receiver = place_ends(jax.random.randint(arg_keys[8], (MEDGES,), 0, MESH_P), jax.random.fold_in(arg_keys[8], 1), 0, MESH_P - 1).astype(jnp.int32)
    mesh_send_node = place_ends(jax.random.randint(arg_keys[9], (N_BLK * N_BAND, N_BLK * MCAP), 0, MESH_P), jax.random.fold_in(arg_keys[9], 1), 0, MESH_P - 1).astype(jnp.int32)
    grid_weights = scatter_about(arg_keys[10], (2, D, D), D ** -0.5, 0.25)
    enc_edge_weights = scatter_about(arg_keys[11], (4, D, D), D ** -0.5, 0.25)
    enc_node_weights = scatter_about(arg_keys[12], (3, D, D), D ** -0.5, 0.25)
    proc_edge_weights = scatter_about(arg_keys[13], (4, D, D), D ** -0.5, 0.25)
    proc_node_weights = scatter_about(arg_keys[14], (3, D, D), D ** -0.5, 0.25)
    biases = scatter_about(arg_keys[15], (5, 2, D), 0.5, 3.0, (), jnp.float32)
    gains = jnp.clip(1.0 + 0.1 * jax.random.normal(arg_keys[16], (5, D), jnp.float32), 0.5, 1.5)
    return {"grid_nodes": grid_nodes, "enc_edges": enc_edges, "enc_sender": enc_sender, "enc_slot": enc_slot, "enc_slot_node": enc_slot_node, "mesh_nodes": mesh_nodes, "mesh_edges": mesh_edges, "mesh_sender": mesh_sender, "mesh_receiver": mesh_receiver, "mesh_send_node": mesh_send_node, "grid_weights": grid_weights, "enc_edge_weights": enc_edge_weights, "enc_node_weights": enc_node_weights, "proc_edge_weights": proc_edge_weights, "proc_node_weights": proc_node_weights, "biases": biases, "gains": gains}


def layer_norm(values, gain_row):
    center = values - lax.optimization_barrier(jnp.mean(values, axis=-1, keepdims=True))
    spread = lax.optimization_barrier(jnp.mean(center * center, axis=-1, keepdims=True))
    return center * lax.rsqrt(spread + 1e-05) * gain_row

def dense_tail(first_layer, second_weight, bias_pair, gain_row):
    hidden = jax.nn.silu(first_layer + bias_pair[0]).astype(jnp.bfloat16)
    second = jnp.dot(hidden, second_weight, preferred_element_type=jnp.float32) + bias_pair[1]
    return layer_norm(second, gain_row)

def project(node_rows, weight):
    return jnp.dot(node_rows, weight, preferred_element_type=jnp.float32)

def reference(grid_nodes, enc_edges, enc_sender, enc_slot, enc_slot_node, mesh_nodes, mesh_edges, mesh_sender, mesh_receiver, mesh_send_node, grid_weights, enc_edge_weights, enc_node_weights, proc_edge_weights, proc_node_weights, biases, gains):
    grid_first = project(grid_nodes, grid_weights[0])
    grid_out = (grid_nodes.astype(jnp.float32) + dense_tail(grid_first, grid_weights[1], biases[0], gains[0])).astype(jnp.bfloat16)
    edge_device = jnp.arange(EDGES, dtype=jnp.int32) // EDGE_DEV
    edge_patch = edge_device // N_BAND
    edge_band = edge_device % N_BAND
    target_patch = (edge_patch + enc_slot // CAP - NEIGH // 2) % N_BLK
    slot_flat = enc_slot_node.reshape(-1)
    slot_index = (target_patch * N_BAND + edge_band) * (NEIGH * CAP) + enc_slot
    target_node = target_patch * MESH_P + slot_flat[slot_index]
    source_node = edge_device * GRID_DEV + enc_sender
    receiver_keys = project(mesh_nodes, enc_edge_weights[2]).astype(jnp.bfloat16)
    sender_proj = project(grid_nodes, enc_edge_weights[1])
    edge_first = project(enc_edges, enc_edge_weights[0]) + sender_proj[source_node] + receiver_keys[target_node].astype(jnp.float32)
    enc_message = dense_tail(edge_first, enc_edge_weights[3], biases[1], gains[1]).astype(jnp.bfloat16)
    enc_sum = jax.ops.segment_sum(enc_message.astype(jnp.float32), target_node, num_segments=MESH)
    node_first = project(mesh_nodes, enc_node_weights[0]) + project(enc_sum.astype(jnp.bfloat16), enc_node_weights[1])
    mesh_mid = (mesh_nodes.astype(jnp.float32) + dense_tail(node_first, enc_node_weights[2], biases[2], gains[2])).astype(jnp.bfloat16)
    mesh_device = jnp.arange(MEDGES, dtype=jnp.int32) // MEDGE_DEV
    mesh_patch = mesh_device // N_BAND
    mesh_band = mesh_device % N_BAND
    source_patch = mesh_sender // MCAP
    send_flat = mesh_send_node.reshape(-1)
    send_index = (source_patch * N_BAND + mesh_band) * (N_BLK * MCAP) + mesh_patch * MCAP + mesh_sender % MCAP
    mesh_source = source_patch * MESH_P + send_flat[send_index]
    mesh_target = mesh_patch * MESH_P + mesh_receiver
    sender_keys = project(mesh_mid, proc_edge_weights[1]).astype(jnp.bfloat16)
    target_keys = project(mesh_mid, proc_edge_weights[2]).astype(jnp.bfloat16)
    mesh_first = project(mesh_edges, proc_edge_weights[0]) + sender_keys[mesh_source].astype(jnp.float32) + target_keys[mesh_target].astype(jnp.float32)
    proc_message = dense_tail(mesh_first, proc_edge_weights[3], biases[3], gains[3]).astype(jnp.bfloat16)
    proc_sum = jax.ops.segment_sum(proc_message.astype(jnp.float32), mesh_target, num_segments=MESH)
    final_first = project(mesh_mid, proc_node_weights[0]) + project(proc_sum.astype(jnp.bfloat16), proc_node_weights[1])
    mesh_out = (mesh_mid.astype(jnp.float32) + dense_tail(final_first, proc_node_weights[2], biases[4], gains[4])).astype(jnp.bfloat16)
    return (grid_out, mesh_out)
```

```python
import jax
import jax.numpy as jnp
from jax import lax
from jax.experimental import pallas as pl
from jax.experimental.pallas import tpu as pltpu
from jax.sharding import PartitionSpec as P

NEIGH = 8
CAP = 64
MIDDLE = NEIGH // 2
WINDOWS = [k for k in range(NEIGH) if k != MIDDLE]
NC = 2
MESH = pl.DeviceIdType.MESH
BF = jnp.bfloat16
F32 = jnp.float32
LANES = 128


def dot(a, b):
    return jnp.dot(a, b, preferred_element_type=F32)


def silu(v):
    half = 0.5 * v
    return half + half * jnp.tanh(half)


def norm(values, gain_row):
    center = values - jnp.mean(values, axis=-1, keepdims=True)
    spread = jnp.mean(center * center, axis=-1, keepdims=True)
    return center * lax.rsqrt(spread + 1e-05) * gain_row


def one_hot(flags):
    return jnp.where(flags, 1.0, 0.0).astype(BF)


def down_column(row):
    return jnp.transpose(jnp.broadcast_to(row, (LANES, LANES)))


def rows_select(column, width, start=0):
    lane = lax.broadcasted_iota(jnp.int32, (LANES, LANES), 1)
    return jnp.concatenate(
        [one_hot(column == lane + (start + j)) for j in range(0, width, LANES)], axis=1
    )


def cols_select(row, height):
    return one_hot(lax.broadcasted_iota(jnp.int32, (height, LANES), 0) == row)


def kernel(
    grid_nodes, enc_edges, enc_sender, enc_slot, enc_slot_node, mesh_nodes, mesh_edges,
    mesh_sender, mesh_receiver, mesh_send_node, grid_w, enc_w, node_w, proc_w, final_w,
    biases, gains,
    grid_out, mesh_out,
    v_grid, v_ee, v_esnd, v_eslot, v_esn, v_mesh, v_me, v_msnd, v_mrcv, v_msn,
    v_gw, v_ew, v_nw, v_pw, v_fw, v_bias, v_gain, v_go, v_mo,
    keys, arrived, ssum, landed, part, far, near, relay, relayed, mid, srows, arr, arr2,
    part2, far2, near2, relay2, relayed2,
    g_key, g_slot, s_slot, g_snd, p_node, g_send, g_msnd, g_rcv, r_rcv,
    sproj, acc, acc2, opart, msg, base_mid, base_fin, gsel, tkeys,
    load_sem, out_sem, ka_s, ka_r, cs_s, cs_r, rs_s, rs_r, ag_s, ag_r, aa_s, aa_r, rt_s, rt_r,
):
    n_blk = lax.axis_size("blk")
    n_band = lax.axis_size("band")
    blk = lax.axis_index("blk")
    band = lax.axis_index("band")
    left = lax.rem(band + n_band - 1, n_band)
    right = lax.rem(band + 1, n_band)
    across = lax.rem(band + 2, n_band)
    width = v_mesh.shape[1]
    wc = width // NC
    nodes = v_mesh.shape[0]
    share = nodes // n_band
    slots = NEIGH * CAP
    edges = v_ee.shape[0]
    medges = v_me.shape[0]
    cols = [slice(c * wc, (c + 1) * wc) for c in range(NC)]

    loads = {}

    def load(name, src, dst):
        copy = pltpu.make_async_copy(src, dst, load_sem.at[len(loads)])
        copy.start()
        loads[name] = copy

    def ready(*names):
        for name in names:
            loads[name].wait()

    load("esn", enc_slot_node, v_esn)
    load("mesh", mesh_nodes, v_mesh)
    load("ew2", enc_w.at[2], v_ew.at[2])

    barrier = pltpu.get_barrier_semaphore()

    @pl.loop(1, n_blk)
    def _(r):
        pl.semaphore_signal(
            barrier, inc=1, device_id=(lax.rem(blk + r, n_blk), band), device_id_type=MESH
        )

    for peer in (left, right):
        pl.semaphore_signal(barrier, inc=1, device_id=(blk, peer), device_id_type=MESH)

    load("grid", grid_nodes, v_grid)
    load("ew1", enc_w.at[1], v_ew.at[1])
    load("esnd", enc_sender, v_esnd)
    load("eslot", enc_slot, v_eslot)
    load("bias", biases, v_bias)
    load("gain", gains, v_gain)
    load("ee", enc_edges, v_ee)
    load("ew0", enc_w.at[0], v_ew.at[0])
    load("ew3", enc_w.at[3], v_ew.at[3])
    load("nw0", node_w.at[0], v_nw.at[0])
    load("nw1", node_w.at[1], v_nw.at[1])
    load("nw2", node_w.at[2], v_nw.at[2])
    load("msn", mesh_send_node, v_msn)
    load("msnd", mesh_sender, v_msnd)
    load("mrcv", mesh_receiver, v_mrcv)
    load("me", mesh_edges, v_me)
    load("pw", proc_w, v_pw)
    load("gw", grid_w, v_gw)
    load("fw", final_w, v_fw)

    def remote(src, dst, send, recv, to_blk, to_band):
        return pltpu.make_async_remote_copy(
            src_ref=src, dst_ref=dst, send_sem=send, recv_sem=recv,
            device_id=(to_blk, to_band), device_id_type=MESH,
        )

    sent = []

    ready("esn")
    for r in range(slots // LANES):
        column = down_column(v_esn[0:1, r * LANES : (r + 1) * LANES])
        g_key[r * LANES : (r + 1) * LANES, :] = rows_select(column, nodes)
    ready("mesh", "ew2")
    gsel[...] = dot(g_key[...], v_mesh[...]).astype(BF)
    key_copies = []
    for c in range(NC):
        projected = dot(gsel[...], v_ew[2, :, cols[c]]).astype(BF)
        keys[c] = projected.reshape(NEIGH, CAP, wc)
        if c == 0:
            pl.semaphore_wait(barrier, n_blk - 1 + 2)
        copies = []
        for i, k in enumerate(WINDOWS):
            copy = remote(
                keys.at[c, k], arrived.at[c, k], ka_s.at[c, i], ka_r.at[c, i],
                lax.rem(blk + MIDDLE - k + n_blk, n_blk), band,
            )
            copy.start()
            copies.append(copy)
        key_copies.append(copies)
        sent += copies
        arrived[c, MIDDLE] = keys[c, MIDDLE]

    ready("grid", "ew1")
    sproj[...] = dot(v_grid[...], v_ew[1]).astype(BF)
    ready("esnd", "eslot")

    @pl.loop(0, edges // LANES)
    def _(r):
        rows = pl.ds(pl.multiple_of(r * LANES, LANES), LANES)
        g_snd[rows, :] = rows_select(down_column(v_esnd[pl.ds(r, 1), :]), v_grid.shape[0])
        slot_row = v_eslot[pl.ds(r, 1), :]
        g_slot[rows, :] = rows_select(down_column(slot_row), slots)
        s_slot[:, rows] = cols_select(slot_row, slots)

    ready("bias", "gain", "ee", "ew0")
    TILE = 256

    @pl.loop(0, edges // TILE)
    def _(t):
        rows = pl.ds(pl.multiple_of(t * TILE, TILE), TILE)
        acc[rows, :] = (
            dot(v_ee[rows, :], v_ew[0]) + dot(g_snd[rows, :], sproj[...]) + v_bias[1, 0:1, :]
        )

    ready("ew3")

    for c in range(NC):
        for copy in key_copies[c]:
            copy.wait_recv()

        @pl.loop(0, edges // TILE)
        def _(t):
            rows = pl.ds(pl.multiple_of(t * TILE, TILE), TILE)
            first = acc[rows, cols[c]] + dot(g_slot[rows, :], arrived[c].reshape(slots, wc))
            second = dot(silu(first).astype(BF), v_ew[3, cols[c], :])
            if c > 0:
                second = second + opart[rows, :]
            if c < NC - 1:
                opart[rows, :] = second
            else:
                msg[rows, :] = norm(second + v_bias[1, 1:2, :], v_gain[1:2, :]).astype(BF)

    sum_copies = []
    for c in range(NC):
        ssum[c] = dot(s_slot[...], msg[:, cols[c]]).astype(BF).reshape(NEIGH, CAP, wc)
        copies = []
        for i, k in enumerate(WINDOWS):
            copy = remote(
                ssum.at[c, k], landed.at[c, k], cs_s.at[c, i], cs_r.at[c, i],
                lax.rem(blk + k - MIDDLE + n_blk, n_blk), band,
            )
            copy.start()
            copies.append(copy)
        sum_copies.append(copies)
        sent += copies
        landed[c, MIDDLE] = ssum[c, MIDDLE]

    for r in range(slots // LANES):
        select = cols_select(v_esn[0:1, r * LANES : (r + 1) * LANES], nodes)
        p_node[:, :, r * LANES : (r + 1) * LANES] = select.reshape(n_band, share, LANES)
    ready("nw0", "nw1", "nw2", "msn", "msnd", "mrcv")
    own_rows = pl.ds(pl.multiple_of(band * share, 32), share)
    base_mid[...] = dot(v_mesh[own_rows, :], v_nw[0]) + v_bias[2, 0:1, :]
    for r in range(v_msn.shape[1] // LANES):
        column = down_column(v_msn[0:1, r * LANES : (r + 1) * LANES])
        g_send[r * LANES : (r + 1) * LANES, :] = rows_select(column, nodes)

    def toward(c):
        return (left, right) if c == 0 else (right, left)

    def scatter_start(c, part, far, near, sem_s, sem_r):
        first, other = toward(c)
        far_copy = remote(part.at[c, across], far.at[c], sem_s.at[c, 0], sem_r.at[c, 0], blk, first)
        near_copy = remote(part.at[c, other], near.at[c], sem_s.at[c, 1], sem_r.at[c, 1], blk, other)
        far_copy.start()
        near_copy.start()
        return far_copy, near_copy

    def scatter_relay(c, far_copy, part, far, relay, relayed, sem_s, sem_r):
        first, _ = toward(c)
        far_copy.wait_recv()
        relay[c] = (far[c].astype(F32) + part[c, first].astype(F32)).astype(BF)
        copy = remote(relay.at[c], relayed.at[c], sem_s.at[c, 2], sem_r.at[c, 2], blk, first)
        copy.start()
        return copy

    scatters = []
    for c in range(NC):
        for copy in sum_copies[c]:
            copy.wait_recv()
        sums = landed[c].reshape(slots, wc)
        for s in range(n_band):
            part[c, s] = dot(p_node[s], sums).astype(BF)
        scatters.append(scatter_start(c, part, far, near, rs_s, rs_r))
    relays = []
    for c in range(NC):
        relays.append(scatter_relay(c, scatters[c][0], part, far, relay, relayed, rs_s, rs_r))
        sent += [*scatters[c], relays[c]]

    first = base_mid[...]
    for c in range(NC):
        scatters[c][1].wait_recv()
        relays[c].wait_recv()
        total = part[c, band].astype(F32) + near[c].astype(F32) + relayed[c].astype(F32)
        first = first + dot(total.astype(BF), v_nw[1, cols[c], :])
    tail = norm(dot(silu(first).astype(BF), v_nw[2]) + v_bias[2, 1:2, :], v_gain[2:3, :])
    own_mid = (v_mesh[own_rows, :].astype(F32) + tail).astype(BF)
    for c in range(NC):
        mid[c, band] = own_mid[:, cols[c]]

    gathers = {}
    for c in range(NC):
        first_peer, other_peer = toward(c)
        for hop, peer in ((0, first_peer), (1, other_peer)):
            gathers[c, hop] = remote(
                mid.at[c, band], mid.at[c, band], ag_s.at[c, hop], ag_r.at[c, hop], blk, peer
            )
    for hop in range(2):
        for c in range(NC):
            gathers[c, hop].start()

    ready("me", "pw")

    @pl.loop(0, medges // LANES)
    def _(r):
        rows = pl.ds(pl.multiple_of(r * LANES, LANES), LANES)
        acc2[rows, :] = dot(v_me[rows, :], v_pw[0]) + v_bias[3, 0:1, :]
        g_msnd[rows, :] = rows_select(down_column(v_msnd[pl.ds(r, 1), :]), slots)

    for c in range(NC):
        first_peer, other_peer = toward(c)
        gathers[c, 0].wait_recv()
        gathers[c, 2] = remote(
            mid.at[c, other_peer], mid.at[c, other_peer], ag_s.at[c, 2], ag_r.at[c, 2], blk, first_peer
        )
        gathers[c, 2].start()
    base_fin[...] = v_bias[4, 0:1, :] + jnp.zeros_like(base_fin)
    requested = None
    for c in range(NC):
        gathers[c, 1].wait_recv()
        gathers[c, 2].wait_recv()
        picked = dot(g_send[...], mid[c].reshape(nodes, wc)).astype(BF)
        term = dot(picked, v_pw[1, cols[c], :])
        requested = term if requested is None else requested + term
    sent += list(gathers.values())
    srows[...] = requested.reshape(srows.shape).astype(BF)

    @pl.loop(0, n_blk - 1)
    def _(i):
        step = (i + 1) // 2
        r = n_blk // 2 + step * (1 - 2 * lax.rem(i, 2))
        to = lax.rem(blk + r, n_blk)
        remote(srows.at[to], arr.at[blk], aa_s, aa_r, to, band).start()

    arr[blk] = srows[blk]

    tk = None
    for c in range(NC):
        term = dot(mid[c].reshape(nodes, wc), v_pw[2, cols[c], :])
        tk = term if tk is None else tk + term
    tkeys[...] = tk.astype(BF)

    @pl.loop(0, medges // LANES)
    def _(r):
        rows = pl.ds(pl.multiple_of(r * LANES, LANES), LANES)
        receiver_row = v_mrcv[pl.ds(r, 1), :]
        select = rows_select(down_column(receiver_row), nodes)
        acc2[rows, :] = acc2[rows, :] + dot(select, tkeys[...])
        r_rcv[:, rows] = cols_select(receiver_row, nodes)

    ready("gw")

    @pl.loop(0, v_grid.shape[0] // TILE)
    def _(t):
        rows = pl.ds(pl.multiple_of(t * TILE, TILE), TILE)
        first = dot(v_grid[rows, :], v_gw[0]) + v_bias[0, 0:1, :]
        tail = norm(dot(silu(first).astype(BF), v_gw[1]) + v_bias[0, 1:2, :], v_gain[0:1, :])
        v_go[rows, :] = (v_grid[rows, :].astype(F32) + tail).astype(BF)

    grid_copy = pltpu.make_async_copy(v_go, grid_out, out_sem.at[0])
    grid_copy.start()
    ready("fw")
    fin = v_bias[4, 0:1, :]
    for c in range(NC):
        fin = fin + dot(mid[c, band], v_fw[0, cols[c], :])
    base_fin[...] = fin

    blocks = pl.ds(0, n_blk - 1)
    everyone = remote(srows.at[blocks], arr.at[blocks], aa_s, aa_r, blk, band)
    everyone.wait_recv()
    arr2[...] = arr[...].astype(F32).reshape(arr2.shape).astype(BF)

    @pl.loop(0, medges // TILE)
    def _(t):
        rows = pl.ds(pl.multiple_of(t * TILE, TILE), TILE)
        first = acc2[rows, :] + dot(g_msnd[rows, :], arr2[...])
        second = dot(silu(first).astype(BF), v_pw[3]) + v_bias[3, 1:2, :]
        msg[rows, :] = norm(second, v_gain[3:4, :]).astype(BF)

    scatters = []
    for c in range(NC):
        sums = dot(r_rcv[...], msg[:, cols[c]]).astype(BF)
        part2[c] = sums.reshape(n_band, share, wc)
        scatters.append(scatter_start(c, part2, far2, near2, rt_s, rt_r))
    relays = []
    for c in range(NC):
        relays.append(scatter_relay(c, scatters[c][0], part2, far2, relay2, relayed2, rt_s, rt_r))
        sent += [*scatters[c], relays[c]]
    first = base_fin[...]
    for c in range(NC):
        scatters[c][1].wait_recv()
        relays[c].wait_recv()
        total = part2[c, band].astype(F32) + near2[c].astype(F32) + relayed2[c].astype(F32)
        first = first + dot(total.astype(BF), v_fw[1, cols[c], :])
    tail = norm(dot(silu(first).astype(BF), v_fw[2]) + v_bias[4, 1:2, :], v_gain[4:5, :])
    for c in range(NC):
        v_mo[:, cols[c]] = (mid[c, band].astype(F32) + tail[:, cols[c]]).astype(BF)
    mesh_copy = pltpu.make_async_copy(v_mo, mesh_out, out_sem.at[1])
    mesh_copy.start()
    for copy in sent:
        copy.wait_send()
    everyone.wait_send()
    grid_copy.wait()
    mesh_copy.wait()


def per_device(n_blk, n_band, *args):
    (grid_nodes, enc_edges, enc_sender, enc_slot, enc_slot_node, mesh_nodes, mesh_edges,
     mesh_sender, mesh_receiver, mesh_send_node, *params) = args

    def folded(index):
        return index.reshape(-1, LANES)

    args = (grid_nodes, enc_edges, folded(enc_sender), folded(enc_slot), enc_slot_node, mesh_nodes,
            mesh_edges, folded(mesh_sender), folded(mesh_receiver), mesh_send_node, *params)
    width = mesh_nodes.shape[1]
    wc = width // NC
    nodes = mesh_nodes.shape[0]
    share = nodes // n_band
    grid_rows = grid_nodes.shape[0]
    edges, medges = enc_edges.shape[0], mesh_edges.shape[0]
    slots = NEIGH * CAP
    requests = mesh_send_node.shape[1]
    vm = pltpu.VMEM
    dma = pltpu.SemaphoreType.DMA
    scratch = [vm(a.shape, a.dtype) for a in args]
    scratch += [vm((grid_rows, width), BF), vm((share, width), BF)]
    window = (NC, NEIGH, CAP, wc)
    shares, piece = (NC, n_band, share, wc), (NC, share, wc)
    boxes = (n_blk, requests // n_blk, width)
    scratch += [vm(window, BF)] * 4
    scratch += [vm(shares, BF)] + [vm(piece, BF)] * 4
    scratch += [vm(shares, BF), vm(boxes, BF), vm(boxes, BF), vm((requests, width), BF)]
    scratch += [vm(shares, BF)] + [vm(piece, BF)] * 4
    scratch += [
        vm((slots, nodes), BF), vm((edges, slots), BF), vm((slots, edges), BF),
        vm((edges, grid_rows), BF), vm((n_band, share, slots), BF), vm((requests, nodes), BF),
        vm((medges, requests), BF), vm((8, LANES), BF), vm((nodes, medges), BF),
    ]
    scratch += [
        vm((grid_rows, width), BF), vm((edges, width), F32), vm((medges, width), F32),
        vm((edges, width), F32), vm((max(edges, medges), width), BF), vm((share, width), F32),
        vm((share, width), F32), vm((slots, width), BF), vm((nodes, width), BF),
    ]
    near = len(WINDOWS)
    scratch += [dma((24,)), dma((2,))]
    scratch += [dma((NC, near))] * 4
    scratch += [dma((NC, 3))] * 4
    scratch += [dma, dma] + [dma((NC, 3))] * 2
    anywhere = pl.BlockSpec(memory_space=pl.ANY)
    return pl.pallas_call(
        kernel,
        out_shape=(
            jax.ShapeDtypeStruct((grid_rows, width), BF),
            jax.ShapeDtypeStruct((share, width), BF),
        ),
        in_specs=[anywhere] * len(args),
        out_specs=(anywhere, anywhere),
        scratch_shapes=scratch,
        compiler_params=pltpu.CompilerParams(
            collective_id=0, has_side_effects=True, vmem_limit_bytes=56 * 1024 * 1024
        ),
        name="encoder_processor",
    )(*args)


def solution(mesh):
    rows = P(("blk", "band"), None)
    flat = P(("blk", "band"))
    in_specs = (rows, rows, flat, flat, rows, P("blk", None), rows, flat, flat, rows) + (P(),) * 7
    n_blk, n_band = mesh.shape["blk"], mesh.shape["band"]

    def step(*args):
        return per_device(n_blk, n_band, *args)

    return jax.shard_map(
        step, mesh=mesh, in_specs=in_specs, out_specs=(rows, rows), check_vma=False
    )
```

```python
import jax
import jax.numpy as jnp
from jax import lax
from jax.experimental import pallas as pl
from jax.experimental.pallas import tpu as pltpu
from jax.sharding import PartitionSpec as P

NEIGH = 8
CAP = 64
MIDDLE = NEIGH // 2
WINDOWS = [k for k in range(NEIGH) if k != MIDDLE]
NC = 2
NS = 4
MESH = pl.DeviceIdType.MESH
BF = jnp.bfloat16
F32 = jnp.float32
LANES = 128


def dot(a, b):
    return jnp.dot(a, b, preferred_element_type=F32)


def silu(v):
    half = 0.5 * v
    return half + half * jnp.tanh(half)


def norm(values, gain_row):
    center = values - jnp.mean(values, axis=-1, keepdims=True)
    spread = jnp.mean(center * center, axis=-1, keepdims=True)
    return center * lax.rsqrt(spread + 1e-05) * gain_row


def one_hot(flags):
    return jnp.where(flags, 1.0, 0.0).astype(BF)


def down_column(row):
    return jnp.transpose(jnp.broadcast_to(row, (LANES, LANES)))


def rows_select(column, width, start=0):
    lane = lax.broadcasted_iota(jnp.int32, (LANES, LANES), 1)
    return jnp.concatenate(
        [one_hot(column == lane + (start + j)) for j in range(0, width, LANES)], axis=1
    )


def cols_select(row, height):
    return one_hot(lax.broadcasted_iota(jnp.int32, (height, LANES), 0) == row)


def kernel(
    grid_nodes, enc_edges, enc_sender, enc_slot, enc_slot_node, mesh_nodes, mesh_edges,
    mesh_sender, mesh_receiver, mesh_send_node, grid_w, enc_w, node_w, proc_w, final_w,
    biases, gains,
    grid_out, mesh_out,
    v_grid, v_ee, v_esnd, v_eslot, v_esn, v_mesh, v_me, v_msnd, v_mrcv, v_msn,
    v_gw, v_ew, v_nw, v_pw, v_fw, v_bias, v_gain, v_go, v_mo,
    keys, arrived, ssum, landed, part, came, mid, srows, arr, arr2,
    part2, far2, near2, relay2, relayed2,
    g_key, g_slot, s_slot, g_snd, p_node, g_send, g_msnd, g_rcv, r_rcv,
    sproj, acc, acc2, opart, msg, base_mid, base_fin, gsel, tkeys,
    load_sem, out_sem, ka_s, ka_r, cs_s, cs_r, rs_s, rs_r, ag_s, ag_r, aa_s, aa_r, rt_s, rt_r,
):
    n_blk = lax.axis_size("blk")
    n_band = lax.axis_size("band")
    blk = lax.axis_index("blk")
    band = lax.axis_index("band")
    left = lax.rem(band + n_band - 1, n_band)
    right = lax.rem(band + 1, n_band)
    across = lax.rem(band + 2, n_band)
    width = v_mesh.shape[1]
    wc = width // NC
    ws = width // NS
    nodes = v_mesh.shape[0]
    share = nodes // n_band
    slots = NEIGH * CAP
    edges = v_ee.shape[0]
    medges = v_me.shape[0]
    cols = [slice(c * wc, (c + 1) * wc) for c in range(NC)]

    loads = {}

    def load(name, src, dst):
        copy = pltpu.make_async_copy(src, dst, load_sem.at[len(loads)])
        copy.start()
        loads[name] = copy

    def ready(*names):
        for name in names:
            loads[name].wait()

    load("esn", enc_slot_node, v_esn)
    load("mesh", mesh_nodes, v_mesh)
    load("ew2", enc_w.at[2], v_ew.at[2])

    barrier = pltpu.get_barrier_semaphore()

    @pl.loop(1, n_blk)
    def _(r):
        pl.semaphore_signal(
            barrier, inc=1, device_id=(lax.rem(blk + r, n_blk), band), device_id_type=MESH
        )

    for peer in (left, right, across):
        pl.semaphore_signal(barrier, inc=1, device_id=(blk, peer), device_id_type=MESH)

    load("grid", grid_nodes, v_grid)
    load("ew1", enc_w.at[1], v_ew.at[1])
    load("esnd", enc_sender, v_esnd)
    load("eslot", enc_slot, v_eslot)
    load("bias", biases, v_bias)
    load("gain", gains, v_gain)
    load("ee", enc_edges, v_ee)
    load("ew0", enc_w.at[0], v_ew.at[0])
    load("ew3", enc_w.at[3], v_ew.at[3])
    load("nw0", node_w.at[0], v_nw.at[0])
    load("nw1", node_w.at[1], v_nw.at[1])
    load("nw2", node_w.at[2], v_nw.at[2])
    load("msn", mesh_send_node, v_msn)
    load("msnd", mesh_sender, v_msnd)
    load("mrcv", mesh_receiver, v_mrcv)
    load("me", mesh_edges, v_me)
    load("pw", proc_w, v_pw)
    load("gw", grid_w, v_gw)
    load("fw", final_w, v_fw)

    def remote(src, dst, send, recv, to_blk, to_band):
        return pltpu.make_async_remote_copy(
            src_ref=src, dst_ref=dst, send_sem=send, recv_sem=recv,
            device_id=(to_blk, to_band), device_id_type=MESH,
        )

    sent = []

    ready("esn")
    for r in range(slots // LANES):
        column = down_column(v_esn[0:1, r * LANES : (r + 1) * LANES])
        g_key[r * LANES : (r + 1) * LANES, :] = rows_select(column, nodes)
    ready("mesh", "ew2")
    gsel[...] = dot(g_key[...], v_mesh[...]).astype(BF)
    key_copies = []
    for c in range(NC):
        projected = dot(gsel[...], v_ew[2, :, cols[c]]).astype(BF)
        keys[c] = projected.reshape(NEIGH, CAP, wc)
        if c == 0:
            pl.semaphore_wait(barrier, n_blk - 1 + n_band - 1)
        copies = []
        for i, k in enumerate(WINDOWS):
            copy = remote(
                keys.at[c, k], arrived.at[c, k], ka_s.at[c, i], ka_r.at[c, i],
                lax.rem(blk + MIDDLE - k + n_blk, n_blk), band,
            )
            copy.start()
            copies.append(copy)
        key_copies.append(copies)
        sent += copies
        arrived[c, MIDDLE] = keys[c, MIDDLE]

    ready("grid", "ew1")
    sproj[...] = dot(v_grid[...], v_ew[1]).astype(BF)
    ready("esnd", "eslot")

    @pl.loop(0, edges // LANES, unroll=2)
    def _(r):
        rows = pl.ds(pl.multiple_of(r * LANES, LANES), LANES)
        g_snd[rows, :] = rows_select(down_column(v_esnd[pl.ds(r, 1), :]), v_grid.shape[0])
        slot_row = v_eslot[pl.ds(r, 1), :]
        g_slot[rows, :] = rows_select(down_column(slot_row), slots)
        s_slot[:, rows] = cols_select(slot_row, slots)

    ready("bias", "gain", "ee", "ew0")
    TILE = 256

    @pl.loop(0, edges // TILE, unroll=True)
    def _(t):
        rows = pl.ds(pl.multiple_of(t * TILE, TILE), TILE)
        acc[rows, :] = (
            dot(v_ee[rows, :], v_ew[0]) + dot(g_snd[rows, :], sproj[...]) + v_bias[1, 0:1, :]
        )

    ready("ew3")

    for c in range(NC):
        for copy in key_copies[c]:
            copy.wait_recv()

        @pl.loop(0, edges // TILE, unroll=True)
        def _(t):
            rows = pl.ds(pl.multiple_of(t * TILE, TILE), TILE)
            first = acc[rows, cols[c]] + dot(g_slot[rows, :], arrived[c].reshape(slots, wc))
            second = dot(silu(first).astype(BF), v_ew[3, cols[c], :])
            if c > 0:
                second = second + opart[rows, :]
            if c < NC - 1:
                opart[rows, :] = second
            else:
                msg[rows, :] = norm(second + v_bias[1, 1:2, :], v_gain[1:2, :]).astype(BF)

    sum_copies = []
    for h in range(NC):
        halves = dot(s_slot[...], msg[:, cols[h]]).astype(BF)
        for c in range(h * NS // NC, (h + 1) * NS // NC):
            low = c * ws - h * wc
            ssum[c] = halves[:, low : low + ws].reshape(NEIGH, CAP, ws)
            copies = []
            for i, k in enumerate(WINDOWS):
                copy = remote(
                    ssum.at[c, k], landed.at[c, k], cs_s.at[c, i], cs_r.at[c, i],
                    lax.rem(blk + k - MIDDLE + n_blk, n_blk), band,
                )
                copy.start()
                copies.append(copy)
            sum_copies.append(copies)
            sent += copies
            landed[c, MIDDLE] = ssum[c, MIDDLE]

    for r in range(slots // LANES):
        select = cols_select(v_esn[0:1, r * LANES : (r + 1) * LANES], nodes)
        p_node[:, r * LANES : (r + 1) * LANES] = select
    ready("nw0", "nw1", "nw2", "msn", "msnd", "mrcv")
    own_rows = pl.ds(pl.multiple_of(band * share, 32), share)
    base_mid[...] = dot(v_mesh[own_rows, :], v_nw[0]) + v_bias[2, 0:1, :]
    for r in range(v_msn.shape[1] // LANES):
        column = down_column(v_msn[0:1, r * LANES : (r + 1) * LANES])
        g_send[r * LANES : (r + 1) * LANES, :] = rows_select(column, nodes)

    def toward(c):
        return (left, right) if c == 0 else (right, left)

    def scatter_start(c, part, far, near, sem_s, sem_r):
        first, other = toward(c)
        far_copy = remote(part.at[c, across], far.at[c], sem_s.at[c, 0], sem_r.at[c, 0], blk, first)
        near_copy = remote(part.at[c, other], near.at[c], sem_s.at[c, 1], sem_r.at[c, 1], blk, other)
        far_copy.start()
        near_copy.start()
        return far_copy, near_copy

    def scatter_relay(c, far_copy, part, far, relay, relayed, sem_s, sem_r):
        first, _ = toward(c)
        far_copy.wait_recv()
        relay[c] = (far[c].astype(F32) + part[c, first].astype(F32)).astype(BF)
        copy = remote(relay.at[c], relayed.at[c], sem_s.at[c, 2], sem_r.at[c, 2], blk, first)
        copy.start()
        return copy

    pieces = []
    for c in range(NS):
        for copy in sum_copies[c]:
            copy.wait_recv()
        sums = dot(p_node[...], landed[c].reshape(slots, ws)).astype(BF)
        part[c] = sums.reshape(n_band, share, ws)
        copies = []
        for i, peer in enumerate((right, left, across)):
            copy = remote(part.at[c, peer], came.at[c, i], rs_s.at[c, i], rs_r.at[c, i], blk, peer)
            copy.start()
            copies.append(copy)
        pieces.append(copies)
        sent += copies

    first = base_mid[...]
    for c in range(NS):
        total = part[c, band].astype(F32)
        for i, copy in enumerate(pieces[c]):
            copy.wait_recv()
            total = total + came[c, i].astype(F32)
        first = first + dot(total.astype(BF), v_nw[1, c * ws : (c + 1) * ws, :])
    tail = norm(dot(silu(first).astype(BF), v_nw[2]) + v_bias[2, 1:2, :], v_gain[2:3, :])
    own_mid = (v_mesh[own_rows, :].astype(F32) + tail).astype(BF)
    for c in range(NC):
        mid[c, band] = own_mid[:, cols[c]]

    gathers = {}
    for c in range(NC):
        first_peer, other_peer = toward(c)
        for hop, peer in ((0, first_peer), (1, other_peer)):
            gathers[c, hop] = remote(
                mid.at[c, band], mid.at[c, band], ag_s.at[c, hop], ag_r.at[c, hop], blk, peer
            )
    for hop in range(2):
        for c in range(NC):
            gathers[c, hop].start()

    for c in range(NC):
        first_peer, other_peer = toward(c)
        gathers[c, 0].wait_recv()
        gathers[c, 2] = remote(
            mid.at[c, other_peer], mid.at[c, other_peer], ag_s.at[c, 2], ag_r.at[c, 2], blk, first_peer
        )
        gathers[c, 2].start()

    ready("me", "pw")

    @pl.loop(0, medges // LANES, unroll=2)
    def _(r):
        rows = pl.ds(pl.multiple_of(r * LANES, LANES), LANES)
        acc2[rows, :] = dot(v_me[rows, :], v_pw[0]) + v_bias[3, 0:1, :]
        g_msnd[rows, :] = rows_select(down_column(v_msnd[pl.ds(r, 1), :]), slots)

    requested = None
    for c in range(NC):
        gathers[c, 1].wait_recv()
        gathers[c, 2].wait_recv()
        picked = dot(g_send[...], mid[c].reshape(nodes, wc)).astype(BF)
        term = dot(picked, v_pw[1, cols[c], :])
        requested = term if requested is None else requested + term
    sent += list(gathers.values())
    srows[...] = requested.reshape(srows.shape).astype(BF)

    @pl.loop(0, n_blk - 1)
    def _(i):
        step = (i + 1) // 2
        r = n_blk // 2 + step * (1 - 2 * lax.rem(i, 2))
        to = lax.rem(blk + r, n_blk)
        remote(srows.at[to], arr.at[blk], aa_s, aa_r, to, band).start()

    arr[blk] = srows[blk]

    tk = None
    for c in range(NC):
        term = dot(mid[c].reshape(nodes, wc), v_pw[2, cols[c], :])
        tk = term if tk is None else tk + term
    tkeys[...] = tk.astype(BF)

    @pl.loop(0, medges // LANES, unroll=2)
    def _(r):
        rows = pl.ds(pl.multiple_of(r * LANES, LANES), LANES)
        receiver_row = v_mrcv[pl.ds(r, 1), :]
        select = rows_select(down_column(receiver_row), nodes)
        acc2[rows, :] = acc2[rows, :] + dot(select, tkeys[...])
        r_rcv[:, rows] = cols_select(receiver_row, nodes)

    ready("gw")

    @pl.loop(0, v_grid.shape[0] // TILE, unroll=True)
    def _(t):
        rows = pl.ds(pl.multiple_of(t * TILE, TILE), TILE)
        first = dot(v_grid[rows, :], v_gw[0]) + v_bias[0, 0:1, :]
        tail = norm(dot(silu(first).astype(BF), v_gw[1]) + v_bias[0, 1:2, :], v_gain[0:1, :])
        v_go[rows, :] = (v_grid[rows, :].astype(F32) + tail).astype(BF)

    grid_copy = pltpu.make_async_copy(v_go, grid_out, out_sem.at[0])
    grid_copy.start()
    ready("fw")
    fin = v_bias[4, 0:1, :]
    for c in range(NC):
        fin = fin + dot(mid[c, band], v_fw[0, cols[c], :])
    base_fin[...] = fin

    blocks = pl.ds(0, n_blk - 1)
    everyone = remote(srows.at[blocks], arr.at[blocks], aa_s, aa_r, blk, band)
    everyone.wait_recv()
    arr2[...] = arr[...].astype(F32).reshape(arr2.shape).astype(BF)

    @pl.loop(0, medges // TILE, unroll=True)
    def _(t):
        rows = pl.ds(pl.multiple_of(t * TILE, TILE), TILE)
        first = acc2[rows, :] + dot(g_msnd[rows, :], arr2[...])
        second = dot(silu(first).astype(BF), v_pw[3]) + v_bias[3, 1:2, :]
        msg[rows, :] = norm(second, v_gain[3:4, :]).astype(BF)

    scatters = []
    for c in range(NC):
        sums = dot(r_rcv[...], msg[:, cols[c]]).astype(BF)
        part2[c] = sums.reshape(n_band, share, wc)
        scatters.append(scatter_start(c, part2, far2, near2, rt_s, rt_r))
    relays = []
    for c in range(NC):
        relays.append(scatter_relay(c, scatters[c][0], part2, far2, relay2, relayed2, rt_s, rt_r))
        sent += [*scatters[c], relays[c]]
    first = base_fin[...]
    for c in range(NC):
        scatters[c][1].wait_recv()
        relays[c].wait_recv()
        total = part2[c, band].astype(F32) + near2[c].astype(F32) + relayed2[c].astype(F32)
        first = first + dot(total.astype(BF), v_fw[1, cols[c], :])
    tail = norm(dot(silu(first).astype(BF), v_fw[2]) + v_bias[4, 1:2, :], v_gain[4:5, :])
    for c in range(NC):
        v_mo[:, cols[c]] = (mid[c, band].astype(F32) + tail[:, cols[c]]).astype(BF)
    mesh_copy = pltpu.make_async_copy(v_mo, mesh_out, out_sem.at[1])
    mesh_copy.start()
    for copy in sent:
        copy.wait_send()
    everyone.wait_send()
    grid_copy.wait()
    mesh_copy.wait()


def handed_on(grid_in, mesh_in, grid_out, mesh_out, v_mesh, v_grid, sem):
    pieces = v_grid.shape[0]
    rows = v_grid.shape[1]
    copies = [(mesh_in, v_mesh, mesh_out)]
    for i in range(pieces):
        part = pl.ds(i * rows, rows)
        copies.append((grid_in.at[part], v_grid.at[i], grid_out.at[part]))
    come = [pltpu.make_async_copy(a, v, sem.at[0, i]) for i, (a, v, _) in enumerate(copies)]
    leave = [pltpu.make_async_copy(v, b, sem.at[1, i]) for i, (_, v, b) in enumerate(copies)]
    for copy in come:
        copy.start()
    for first, second in zip(come, leave):
        first.wait()
        second.start()
    for copy in leave:
        copy.wait()


def per_device(n_blk, n_band, *args):
    (grid_nodes, enc_edges, enc_sender, enc_slot, enc_slot_node, mesh_nodes, mesh_edges,
     mesh_sender, mesh_receiver, mesh_send_node, *params) = args

    def folded(index):
        return index.reshape(-1, LANES)

    args = (grid_nodes, enc_edges, folded(enc_sender), folded(enc_slot), enc_slot_node, mesh_nodes,
            mesh_edges, folded(mesh_sender), folded(mesh_receiver), mesh_send_node, *params)
    width = mesh_nodes.shape[1]
    wc = width // NC
    nodes = mesh_nodes.shape[0]
    share = nodes // n_band
    grid_rows = grid_nodes.shape[0]
    edges, medges = enc_edges.shape[0], mesh_edges.shape[0]
    slots = NEIGH * CAP
    requests = mesh_send_node.shape[1]
    vm = pltpu.VMEM
    dma = pltpu.SemaphoreType.DMA
    scratch = [vm(a.shape, a.dtype) for a in args]
    scratch += [vm((grid_rows, width), BF), vm((share, width), BF)]
    window = (NC, NEIGH, CAP, wc)
    shares, piece = (NC, n_band, share, wc), (NC, share, wc)
    boxes = (n_blk, requests // n_blk, width)
    ws = width // NS
    scratch += [vm(window, BF)] * 2 + [vm((NS, NEIGH, CAP, ws), BF)] * 2
    scratch += [vm((NS, n_band, share, ws), BF), vm((NS, n_band - 1, share, ws), BF)]
    scratch += [vm(shares, BF), vm(boxes, BF), vm(boxes, BF), vm((requests, width), BF)]
    scratch += [vm(shares, BF)] + [vm(piece, BF)] * 4
    scratch += [
        vm((slots, nodes), BF), vm((edges, slots), BF), vm((slots, edges), BF),
        vm((edges, grid_rows), BF), vm((nodes, slots), BF), vm((requests, nodes), BF),
        vm((medges, requests), BF), vm((8, LANES), BF), vm((nodes, medges), BF),
    ]
    scratch += [
        vm((grid_rows, width), BF), vm((edges, width), F32), vm((medges, width), F32),
        vm((edges, width), F32), vm((max(edges, medges), width), BF), vm((share, width), F32),
        vm((share, width), F32), vm((slots, width), BF), vm((nodes, width), BF),
    ]
    near = len(WINDOWS)
    scratch += [dma((24,)), dma((2,))]
    scratch += [dma((NC, near))] * 2 + [dma((NS, near))] * 2
    scratch += [dma((NS, 3))] * 2 + [dma((NC, 3))] * 2
    scratch += [dma, dma] + [dma((NC, 3))] * 2
    anywhere = pl.BlockSpec(memory_space=pl.ANY)
    results = pl.pallas_call(
        kernel,
        out_shape=(
            jax.ShapeDtypeStruct((grid_rows, width), BF),
            jax.ShapeDtypeStruct((share, width), BF),
        ),
        in_specs=[anywhere] * len(args),
        out_specs=(anywhere, anywhere),
        scratch_shapes=scratch,
        compiler_params=pltpu.CompilerParams(
            collective_id=0, has_side_effects=True, vmem_limit_bytes=56 * 1024 * 1024
        ),
        name="encoder_processor",
    )(*args)
    return pl.pallas_call(
        handed_on,
        out_shape=tuple(jax.ShapeDtypeStruct(r.shape, r.dtype) for r in results),
        in_specs=[anywhere] * 2,
        out_specs=(anywhere, anywhere),
        scratch_shapes=[vm((share, width), BF), vm((4, grid_rows // 4, width), BF), dma((2, 5))],
        name="handed_on",
    )(*results)


def solution(mesh):
    rows = P(("blk", "band"), None)
    flat = P(("blk", "band"))
    in_specs = (rows, rows, flat, flat, rows, P("blk", None), rows, flat, flat, rows) + (P(),) * 7
    n_blk, n_band = mesh.shape["blk"], mesh.shape["band"]

    def step(*args):
        return per_device(n_blk, n_band, *args)

    return jax.shard_map(
        step, mesh=mesh, in_specs=in_specs, out_specs=(rows, rows), check_vma=False
    )
```

```python
import jax
import jax.numpy as jnp
from jax import lax
from jax.experimental import pallas as pl
from jax.experimental.pallas import tpu as pltpu
from jax.sharding import PartitionSpec as P

NEIGH = 8
CAP = 64
MIDDLE = NEIGH // 2
WINDOWS = [k for k in range(NEIGH) if k != MIDDLE]
NC = 2
NS = 4
NM = 4
MESH = pl.DeviceIdType.MESH
BF = jnp.bfloat16
F32 = jnp.float32
LANES = 128


def dot(a, b):
    return jnp.dot(a, b, preferred_element_type=F32)


def silu(v):
    half = 0.5 * v
    return half + half * jnp.tanh(half)


def norm(values, gain_row):
    center = values - jnp.mean(values, axis=-1, keepdims=True)
    spread = jnp.mean(center * center, axis=-1, keepdims=True)
    return center * lax.rsqrt(spread + 1e-05) * gain_row


def one_hot(flags):
    return jnp.where(flags, 1.0, 0.0).astype(BF)


def down_column(row):
    return jnp.transpose(jnp.broadcast_to(row, (LANES, LANES)))


def rows_select(column, width, start=0):
    lane = lax.broadcasted_iota(jnp.int32, (LANES, LANES), 1)
    return jnp.concatenate(
        [one_hot(column == lane + (start + j)) for j in range(0, width, LANES)], axis=1
    )


def cols_select(row, height):
    return one_hot(lax.broadcasted_iota(jnp.int32, (height, LANES), 0) == row)


def kernel(
    grid_nodes, enc_edges, enc_sender, enc_slot, enc_slot_node, mesh_nodes, mesh_edges,
    mesh_sender, mesh_receiver, mesh_send_node, grid_w, enc_w, node_w, proc_w, final_w,
    biases, gains,
    grid_out, mesh_out,
    v_grid, v_ee, v_esnd, v_eslot, v_esn, v_mesh, v_me, v_msnd, v_mrcv, v_msn,
    v_gw, v_ew, v_nw, v_pw, v_fw, v_bias, v_gain, v_go, v_mo,
    keys, arrived, ssum, landed, part, came, mid, srows, arr, arr2,
    part2, far2, near2, relay2, relayed2,
    g_key, g_slot, s_slot, g_snd, p_node, g_send, g_msnd, g_rcv, r_rcv,
    sproj, acc, acc2, opart, msg, base_mid, base_fin, gsel, tkeys,
    load_sem, out_sem, ka_s, ka_r, cs_s, cs_r, rs_s, rs_r, ag_s, ag_r, aa_s, aa_r, rt_s, rt_r,
):
    n_blk = lax.axis_size("blk")
    n_band = lax.axis_size("band")
    blk = lax.axis_index("blk")
    band = lax.axis_index("band")
    left = lax.rem(band + n_band - 1, n_band)
    right = lax.rem(band + 1, n_band)
    across = lax.rem(band + 2, n_band)
    width = v_mesh.shape[1]
    wc = width // NC
    ws = width // NS
    wm = width // NM
    nodes = v_mesh.shape[0]
    share = nodes // n_band
    slots = NEIGH * CAP
    edges = v_ee.shape[0]
    medges = v_me.shape[0]
    cols = [slice(c * wc, (c + 1) * wc) for c in range(NC)]

    loads = {}

    def load(name, src, dst):
        copy = pltpu.make_async_copy(src, dst, load_sem.at[len(loads)])
        copy.start()
        loads[name] = copy

    def ready(*names):
        for name in names:
            loads[name].wait()

    load("esn", enc_slot_node, v_esn)
    load("mesh", mesh_nodes, v_mesh)
    load("ew2", enc_w.at[2], v_ew.at[2])

    barrier = pltpu.get_barrier_semaphore()

    @pl.loop(1, n_blk)
    def _(r):
        pl.semaphore_signal(
            barrier, inc=1, device_id=(lax.rem(blk + r, n_blk), band), device_id_type=MESH
        )

    for peer in (left, right, across):
        pl.semaphore_signal(barrier, inc=1, device_id=(blk, peer), device_id_type=MESH)

    load("grid", grid_nodes, v_grid)
    load("ew1", enc_w.at[1], v_ew.at[1])
    load("esnd", enc_sender, v_esnd)
    load("eslot", enc_slot, v_eslot)
    load("bias", biases, v_bias)
    load("gain", gains, v_gain)
    load("ee", enc_edges, v_ee)
    load("ew0", enc_w.at[0], v_ew.at[0])
    load("ew3", enc_w.at[3], v_ew.at[3])
    load("nw0", node_w.at[0], v_nw.at[0])
    load("nw1", node_w.at[1], v_nw.at[1])
    load("nw2", node_w.at[2], v_nw.at[2])
    load("msn", mesh_send_node, v_msn)
    load("msnd", mesh_sender, v_msnd)
    load("mrcv", mesh_receiver, v_mrcv)
    load("me", mesh_edges, v_me)
    load("pw", proc_w, v_pw)
    load("gw", grid_w, v_gw)
    load("fw", final_w, v_fw)

    def remote(src, dst, send, recv, to_blk, to_band):
        return pltpu.make_async_remote_copy(
            src_ref=src, dst_ref=dst, send_sem=send, recv_sem=recv,
            device_id=(to_blk, to_band), device_id_type=MESH,
        )

    sent = []

    ready("esn")
    for r in range(slots // LANES):
        column = down_column(v_esn[0:1, r * LANES : (r + 1) * LANES])
        g_key[r * LANES : (r + 1) * LANES, :] = rows_select(column, nodes)
    ready("mesh", "ew2")
    gsel[...] = dot(g_key[...], v_mesh[...]).astype(BF)
    key_copies = []
    for c in range(NC):
        projected = dot(gsel[...], v_ew[2, :, cols[c]]).astype(BF)
        keys[c] = projected.reshape(NEIGH, CAP, wc)
        if c == 0:
            pl.semaphore_wait(barrier, n_blk - 1 + n_band - 1)
        copies = []
        for i, k in enumerate(WINDOWS):
            copy = remote(
                keys.at[c, k], arrived.at[c, k], ka_s.at[c, i], ka_r.at[c, i],
                lax.rem(blk + MIDDLE - k + n_blk, n_blk), band,
            )
            copy.start()
            copies.append(copy)
        key_copies.append(copies)
        sent += copies
        arrived[c, MIDDLE] = keys[c, MIDDLE]

    ready("grid", "ew1")
    sproj[...] = dot(v_grid[...], v_ew[1]).astype(BF)
    ready("esnd", "eslot")

    @pl.loop(0, edges // LANES, unroll=2)
    def _(r):
        rows = pl.ds(pl.multiple_of(r * LANES, LANES), LANES)
        g_snd[rows, :] = rows_select(down_column(v_esnd[pl.ds(r, 1), :]), v_grid.shape[0])
        slot_row = v_eslot[pl.ds(r, 1), :]
        g_slot[rows, :] = rows_select(down_column(slot_row), slots)
        s_slot[:, rows] = cols_select(slot_row, slots)

    ready("bias", "gain", "ee", "ew0")
    TILE = 256

    @pl.loop(0, edges // TILE, unroll=True)
    def _(t):
        rows = pl.ds(pl.multiple_of(t * TILE, TILE), TILE)
        acc[rows, :] = (
            dot(v_ee[rows, :], v_ew[0]) + dot(g_snd[rows, :], sproj[...]) + v_bias[1, 0:1, :]
        )

    ready("ew3")

    for c in range(NC):
        for copy in key_copies[c]:
            copy.wait_recv()

        @pl.loop(0, edges // TILE, unroll=True)
        def _(t):
            rows = pl.ds(pl.multiple_of(t * TILE, TILE), TILE)
            first = acc[rows, cols[c]] + dot(g_slot[rows, :], arrived[c].reshape(slots, wc))
            second = dot(silu(first).astype(BF), v_ew[3, cols[c], :])
            if c > 0:
                second = second + opart[rows, :]
            if c < NC - 1:
                opart[rows, :] = second
            else:
                msg[rows, :] = norm(second + v_bias[1, 1:2, :], v_gain[1:2, :]).astype(BF)

    sum_copies = []
    for h in range(NC):
        halves = dot(s_slot[...], msg[:, cols[h]]).astype(BF)
        for c in range(h * NS // NC, (h + 1) * NS // NC):
            low = c * ws - h * wc
            ssum[c] = halves[:, low : low + ws].reshape(NEIGH, CAP, ws)
            copies = []
            for i, k in enumerate(WINDOWS):
                copy = remote(
                    ssum.at[c, k], landed.at[c, k], cs_s.at[c, i], cs_r.at[c, i],
                    lax.rem(blk + k - MIDDLE + n_blk, n_blk), band,
                )
                copy.start()
                copies.append(copy)
            sum_copies.append(copies)
            sent += copies
            landed[c, MIDDLE] = ssum[c, MIDDLE]

    for r in range(slots // LANES):
        select = cols_select(v_esn[0:1, r * LANES : (r + 1) * LANES], nodes)
        p_node[:, r * LANES : (r + 1) * LANES] = select
    ready("nw0", "nw1", "nw2", "msn", "msnd", "mrcv", "me", "pw")
    own_rows = pl.ds(pl.multiple_of(band * share, 32), share)

    def fill_base():
        base_mid[...] = dot(v_mesh[own_rows, :], v_nw[0]) + v_bias[2, 0:1, :]

    def fill_send():
        for r in range(v_msn.shape[1] // LANES):
            column = down_column(v_msn[0:1, r * LANES : (r + 1) * LANES])
            g_send[r * LANES : (r + 1) * LANES, :] = rows_select(column, nodes)

    def fill_edges(part, parts):
        count = medges // LANES // parts

        @pl.loop(part * count, (part + 1) * count, unroll=2)
        def _(r):
            rows = pl.ds(pl.multiple_of(r * LANES, LANES), LANES)
            acc2[rows, :] = dot(v_me[rows, :], v_pw[0]) + v_bias[3, 0:1, :]
            g_msnd[rows, :] = rows_select(down_column(v_msnd[pl.ds(r, 1), :]), slots)

    fills = [fill_base, fill_send, lambda: fill_edges(0, 2), lambda: fill_edges(1, 2)]

    def toward(c):
        return (left, right) if c == 0 else (right, left)

    def scatter_start(c, part, far, near, sem_s, sem_r):
        first, other = toward(c)
        far_copy = remote(part.at[c, across], far.at[c], sem_s.at[c, 0], sem_r.at[c, 0], blk, first)
        near_copy = remote(part.at[c, other], near.at[c], sem_s.at[c, 1], sem_r.at[c, 1], blk, other)
        far_copy.start()
        near_copy.start()
        return far_copy, near_copy

    def scatter_relay(c, far_copy, part, far, relay, relayed, sem_s, sem_r):
        first, _ = toward(c)
        far_copy.wait_recv()
        relay[c] = (far[c].astype(F32) + part[c, first].astype(F32)).astype(BF)
        copy = remote(relay.at[c], relayed.at[c], sem_s.at[c, 2], sem_r.at[c, 2], blk, first)
        copy.start()
        return copy

    pieces = []
    for c in range(NS):
        for copy in sum_copies[c]:
            copy.wait_recv()
        sums = dot(p_node[...], landed[c].reshape(slots, ws)).astype(BF)
        part[c] = sums.reshape(n_band, share, ws)
        copies = []
        for i, peer in enumerate((right, left, across)):
            copy = remote(part.at[c, peer], came.at[c, i], rs_s.at[c, i], rs_r.at[c, i], blk, peer)
            copy.start()
            copies.append(copy)
        pieces.append(copies)
        sent += copies
        if c < NS - 1:
            fills[c]()

    first = base_mid[...]
    for c in range(NS):
        total = part[c, band].astype(F32)
        for i, copy in enumerate(pieces[c]):
            copy.wait_recv()
            total = total + came[c, i].astype(F32)
        first = first + dot(total.astype(BF), v_nw[1, c * ws : (c + 1) * ws, :])
    tail = norm(dot(silu(first).astype(BF), v_nw[2]) + v_bias[2, 1:2, :], v_gain[2:3, :])
    own_mid = (v_mesh[own_rows, :].astype(F32) + tail).astype(BF)
    mid[band] = own_mid

    gathers = {}

    def spread(m, hop):
        first_peer, other_peer = toward(m % 2)
        owner = other_peer if hop == 2 else band
        block = mid.at[owner, :, m * wm : (m + 1) * wm]
        gathers[m, hop] = remote(
            block, block, ag_s.at[m, hop], ag_r.at[m, hop], blk, other_peer if hop == 1 else first_peer
        )
        gathers[m, hop].start()

    def spread_own(half):
        for hop in range(2):
            for m in half:
                spread(m, hop)

    def spread_on(half):
        for m in half:
            gathers[m, 0].wait_recv()
            spread(m, 2)

    def pick(h, half):
        for m in half:
            gathers[m, 1].wait_recv()
            gathers[m, 2].wait_recv()
        picked = dot(g_send[...], mid[:, :, cols[h]].reshape(nodes, wc))
        srows[h] = picked.reshape(srows.shape[1:]).astype(BF)

    def to_everyone(h):
        @pl.loop(0, n_blk - 1)
        def _(i):
            step = (i + 1) // 2
            r = n_blk // 2 + step * (1 - 2 * lax.rem(i, 2))
            to = lax.rem(blk + r, n_blk)
            remote(srows.at[h, to], arr.at[h, blk], aa_s.at[h], aa_r.at[h], to, band).start()

        arr[h, blk] = srows[h, blk]

    halves = [range(h * NM // NC, (h + 1) * NM // NC) for h in range(NC)]
    spread_own(halves[0])
    spread_on(halves[0])
    spread_own(halves[1])
    pick(0, halves[0])
    spread_on(halves[1])
    to_everyone(0)
    pick(1, halves[1])
    to_everyone(1)
    fills[NS - 1]()
    sent += list(gathers.values())

    tkeys[...] = dot(mid[...].reshape(nodes, width), v_pw[2]).astype(BF)

    @pl.loop(0, medges // LANES, unroll=2)
    def _(r):
        rows = pl.ds(pl.multiple_of(r * LANES, LANES), LANES)
        receiver_row = v_mrcv[pl.ds(r, 1), :]
        select = rows_select(down_column(receiver_row), nodes)
        acc2[rows, :] = acc2[rows, :] + dot(select, tkeys[...])
        r_rcv[:, rows] = cols_select(receiver_row, nodes)

    ready("gw")

    @pl.loop(0, v_grid.shape[0] // TILE, unroll=True)
    def _(t):
        rows = pl.ds(pl.multiple_of(t * TILE, TILE), TILE)
        first = dot(v_grid[rows, :], v_gw[0]) + v_bias[0, 0:1, :]
        tail = norm(dot(silu(first).astype(BF), v_gw[1]) + v_bias[0, 1:2, :], v_gain[0:1, :])
        v_go[rows, :] = (v_grid[rows, :].astype(F32) + tail).astype(BF)

    grid_copy = pltpu.make_async_copy(v_go, grid_out, out_sem.at[0])
    grid_copy.start()
    ready("fw")
    base_fin[...] = dot(mid[band], v_fw[0]) + v_bias[4, 0:1, :]

    blocks = pl.ds(0, n_blk - 1)
    everyone = [
        remote(srows.at[h, blocks], arr.at[h, blocks], aa_s.at[h], aa_r.at[h], blk, band)
        for h in range(NC)
    ]
    requested = None
    for h in range(NC):
        everyone[h].wait_recv()
        raw = arr[h].astype(F32).reshape(arr2.shape[0], wc).astype(BF)
        term = dot(raw, v_pw[1, cols[h], :])
        if h < NC - 1:
            opart[0 : arr2.shape[0], :] = term if requested is None else opart[0 : arr2.shape[0], :] + term
            requested = opart
        else:
            arr2[...] = (opart[0 : arr2.shape[0], :] + term).astype(BF)

    @pl.loop(0, medges // TILE, unroll=True)
    def _(t):
        rows = pl.ds(pl.multiple_of(t * TILE, TILE), TILE)
        first = acc2[rows, :] + dot(g_msnd[rows, :], arr2[...])
        second = dot(silu(first).astype(BF), v_pw[3]) + v_bias[3, 1:2, :]
        msg[rows, :] = norm(second, v_gain[3:4, :]).astype(BF)

    scatters = []
    for c in range(NC):
        sums = dot(r_rcv[...], msg[:, cols[c]]).astype(BF)
        part2[c] = sums.reshape(n_band, share, wc)
        scatters.append(scatter_start(c, part2, far2, near2, rt_s, rt_r))
    relays = []
    for c in range(NC):
        relays.append(scatter_relay(c, scatters[c][0], part2, far2, relay2, relayed2, rt_s, rt_r))
        sent += [*scatters[c], relays[c]]
    first = base_fin[...]
    for c in range(NC):
        scatters[c][1].wait_recv()
        relays[c].wait_recv()
        total = part2[c, band].astype(F32) + near2[c].astype(F32) + relayed2[c].astype(F32)
        first = first + dot(total.astype(BF), v_fw[1, cols[c], :])
    tail = norm(dot(silu(first).astype(BF), v_fw[2]) + v_bias[4, 1:2, :], v_gain[4:5, :])
    for c in range(NC):
        v_mo[:, cols[c]] = (mid[band, :, cols[c]].astype(F32) + tail[:, cols[c]]).astype(BF)
    mesh_copy = pltpu.make_async_copy(v_mo, mesh_out, out_sem.at[1])
    mesh_copy.start()
    for copy in sent:
        copy.wait_send()
    for copy in everyone:
        copy.wait_send()
    grid_copy.wait()
    mesh_copy.wait()


def handed_on(grid_in, mesh_in, grid_out, mesh_out, v_mesh, v_grid, sem):
    pieces = v_grid.shape[0]
    rows = v_grid.shape[1]
    copies = [(mesh_in, v_mesh, mesh_out)]
    for i in range(pieces):
        part = pl.ds(i * rows, rows)
        copies.append((grid_in.at[part], v_grid.at[i], grid_out.at[part]))
    come = [pltpu.make_async_copy(a, v, sem.at[0, i]) for i, (a, v, _) in enumerate(copies)]
    leave = [pltpu.make_async_copy(v, b, sem.at[1, i]) for i, (_, v, b) in enumerate(copies)]
    for copy in come:
        copy.start()
    for first, second in zip(come, leave):
        first.wait()
        second.start()
    for copy in leave:
        copy.wait()


def per_device(n_blk, n_band, *args):
    (grid_nodes, enc_edges, enc_sender, enc_slot, enc_slot_node, mesh_nodes, mesh_edges,
     mesh_sender, mesh_receiver, mesh_send_node, *params) = args

    def folded(index):
        return index.reshape(-1, LANES)

    args = (grid_nodes, enc_edges, folded(enc_sender), folded(enc_slot), enc_slot_node, mesh_nodes,
            mesh_edges, folded(mesh_sender), folded(mesh_receiver), mesh_send_node, *params)
    width = mesh_nodes.shape[1]
    wc = width // NC
    nodes = mesh_nodes.shape[0]
    share = nodes // n_band
    grid_rows = grid_nodes.shape[0]
    edges, medges = enc_edges.shape[0], mesh_edges.shape[0]
    slots = NEIGH * CAP
    requests = mesh_send_node.shape[1]
    vm = pltpu.VMEM
    dma = pltpu.SemaphoreType.DMA
    scratch = [vm(a.shape, a.dtype) for a in args]
    scratch += [vm((grid_rows, width), BF), vm((share, width), BF)]
    window = (NC, NEIGH, CAP, wc)
    shares, piece = (NC, n_band, share, wc), (NC, share, wc)
    boxes = (NC, n_blk, requests // n_blk, wc)
    ws = width // NS
    scratch += [vm(window, BF)] * 2 + [vm((NS, NEIGH, CAP, ws), BF)] * 2
    scratch += [vm((NS, n_band, share, ws), BF), vm((NS, n_band - 1, share, ws), BF)]
    scratch += [vm((n_band, share, width), BF), vm(boxes, BF), vm(boxes, BF), vm((requests, width), BF)]
    scratch += [vm(shares, BF)] + [vm(piece, BF)] * 4
    scratch += [
        vm((slots, nodes), BF), vm((edges, slots), BF), vm((slots, edges), BF),
        vm((edges, grid_rows), BF), vm((nodes, slots), BF), vm((requests, nodes), BF),
        vm((medges, requests), BF), vm((8, LANES), BF), vm((nodes, medges), BF),
    ]
    scratch += [
        vm((grid_rows, width), BF), vm((edges, width), F32), vm((medges, width), F32),
        vm((edges, width), F32), vm((max(edges, medges), width), BF), vm((share, width), F32),
        vm((share, width), F32), vm((slots, width), BF), vm((nodes, width), BF),
    ]
    near = len(WINDOWS)
    scratch += [dma((24,)), dma((2,))]
    scratch += [dma((NC, near))] * 2 + [dma((NS, near))] * 2
    scratch += [dma((NS, 3))] * 2 + [dma((NM, 3))] * 2
    scratch += [dma((NC,))] * 2 + [dma((NC, 3))] * 2
    anywhere = pl.BlockSpec(memory_space=pl.ANY)
    results = pl.pallas_call(
        kernel,
        out_shape=(
            jax.ShapeDtypeStruct((grid_rows, width), BF),
            jax.ShapeDtypeStruct((share, width), BF),
        ),
        in_specs=[anywhere] * len(args),
        out_specs=(anywhere, anywhere),
        scratch_shapes=scratch,
        compiler_params=pltpu.CompilerParams(
            collective_id=0, has_side_effects=True, vmem_limit_bytes=56 * 1024 * 1024
        ),
        name="encoder_processor",
    )(*args)
    return pl.pallas_call(
        handed_on,
        out_shape=tuple(jax.ShapeDtypeStruct(r.shape, r.dtype) for r in results),
        in_specs=[anywhere] * 2,
        out_specs=(anywhere, anywhere),
        scratch_shapes=[vm((share, width), BF), vm((4, grid_rows // 4, width), BF), dma((2, 5))],
        name="handed_on",
    )(*results)


def solution(mesh):
    rows = P(("blk", "band"), None)
    flat = P(("blk", "band"))
    in_specs = (rows, rows, flat, flat, rows, P("blk", None), rows, flat, flat, rows) + (P(),) * 7
    n_blk, n_band = mesh.shape["blk"], mesh.shape["band"]

    def step(*args):
        return per_device(n_blk, n_band, *args)

    return jax.shard_map(
        step, mesh=mesh, in_specs=in_specs, out_specs=(rows, rows), check_vma=False
    )
```

```python
import jax
import jax.numpy as jnp
from jax import lax
from jax.experimental import pallas as pl
from jax.experimental.pallas import tpu as pltpu
from jax.sharding import PartitionSpec as P

NEIGH = 8
CAP = 64
MIDDLE = NEIGH // 2
WINDOWS = [k for k in range(NEIGH) if k != MIDDLE]
NC = 2
NS = 4
NM = 4
MESH = pl.DeviceIdType.MESH
BF = jnp.bfloat16
F32 = jnp.float32
LANES = 128


def dot(a, b):
    return jnp.dot(a, b, preferred_element_type=F32)


def silu(v):
    half = 0.5 * v
    return half + half * jnp.tanh(half)


def norm(values, gain_row):
    center = values - jnp.mean(values, axis=-1, keepdims=True)
    spread = jnp.mean(center * center, axis=-1, keepdims=True)
    return center * lax.rsqrt(spread + 1e-05) * gain_row


def one_hot(flags):
    return jnp.where(flags, 1.0, 0.0).astype(BF)


def down_column(row):
    return jnp.transpose(jnp.broadcast_to(row, (LANES, LANES)))


def rows_select(column, width, start=0):
    lane = lax.broadcasted_iota(jnp.int32, (LANES, LANES), 1)
    return jnp.concatenate(
        [one_hot(column == lane + (start + j)) for j in range(0, width, LANES)], axis=1
    )


def cols_select(row, height):
    return one_hot(lax.broadcasted_iota(jnp.int32, (height, LANES), 0) == row)


def kernel(
    grid_nodes, enc_edges, enc_sender, enc_slot, enc_slot_node, mesh_nodes, mesh_edges,
    mesh_sender, mesh_receiver, mesh_send_node, grid_w, enc_w, node_w, proc_w, final_w,
    biases, gains,
    v_go, v_mo,
    v_grid, v_ee, v_esnd, v_eslot, v_esn, v_mesh, v_me, v_msnd, v_mrcv, v_msn,
    v_gw, v_ew, v_nw, v_pw, v_fw, v_bias, v_gain,
    keys, arrived, ssum, landed, part, came, mid, srows, arr, arr2,
    part2, far2, near2, relay2, relayed2,
    g_key, g_slot, s_slot, g_snd, p_node, g_send, g_msnd, g_rcv, r_rcv,
    sproj, acc, acc2, opart, msg, base_mid, base_fin, gsel, tkeys,
    load_sem, ka_s, ka_r, cs_s, cs_r, rs_s, rs_r, ag_s, ag_r, aa_s, aa_r, rt_s, rt_r,
):
    n_blk = lax.axis_size("blk")
    n_band = lax.axis_size("band")
    blk = lax.axis_index("blk")
    band = lax.axis_index("band")
    left = lax.rem(band + n_band - 1, n_band)
    right = lax.rem(band + 1, n_band)
    across = lax.rem(band + 2, n_band)
    width = v_mesh.shape[1]
    wc = width // NC
    ws = width // NS
    wm = width // NM
    nodes = v_mesh.shape[0]
    share = nodes // n_band
    slots = NEIGH * CAP
    edges = v_ee.shape[0]
    medges = v_me.shape[0]
    cols = [slice(c * wc, (c + 1) * wc) for c in range(NC)]

    loads = {}

    def load(name, src, dst):
        copy = pltpu.make_async_copy(src, dst, load_sem.at[len(loads)])
        copy.start()
        loads[name] = copy

    def ready(*names):
        for name in names:
            loads[name].wait()

    load("esn", enc_slot_node, v_esn)
    load("mesh", mesh_nodes, v_mesh)
    load("ew2", enc_w.at[2], v_ew.at[2])

    barrier = pltpu.get_barrier_semaphore()

    @pl.loop(1, n_blk)
    def _(r):
        pl.semaphore_signal(
            barrier, inc=1, device_id=(lax.rem(blk + r, n_blk), band), device_id_type=MESH
        )

    for peer in (left, right, across):
        pl.semaphore_signal(barrier, inc=1, device_id=(blk, peer), device_id_type=MESH)

    load("grid", grid_nodes, v_grid)
    load("ew1", enc_w.at[1], v_ew.at[1])
    load("esnd", enc_sender, v_esnd)
    load("eslot", enc_slot, v_eslot)
    load("bias", biases, v_bias)
    load("gain", gains, v_gain)
    load("ee", enc_edges, v_ee)
    load("ew0", enc_w.at[0], v_ew.at[0])
    load("ew3", enc_w.at[3], v_ew.at[3])
    load("nw0", node_w.at[0], v_nw.at[0])
    load("nw1", node_w.at[1], v_nw.at[1])
    load("nw2", node_w.at[2], v_nw.at[2])
    load("msn", mesh_send_node, v_msn)
    load("msnd", mesh_sender, v_msnd)
    load("mrcv", mesh_receiver, v_mrcv)
    load("me", mesh_edges, v_me)
    load("pw", proc_w, v_pw)
    load("gw", grid_w, v_gw)
    load("fw", final_w, v_fw)

    def remote(src, dst, send, recv, to_blk, to_band):
        return pltpu.make_async_remote_copy(
            src_ref=src, dst_ref=dst, send_sem=send, recv_sem=recv,
            device_id=(to_blk, to_band), device_id_type=MESH,
        )

    sent = []

    ready("esn")
    for r in range(slots // LANES):
        column = down_column(v_esn[0:1, r * LANES : (r + 1) * LANES])
        g_key[r * LANES : (r + 1) * LANES, :] = rows_select(column, nodes)
    ready("mesh", "ew2")
    gsel[...] = dot(g_key[...], v_mesh[...]).astype(BF)
    key_copies = []
    for c in range(NC):
        projected = dot(gsel[...], v_ew[2, :, cols[c]]).astype(BF)
        keys[c] = projected.reshape(NEIGH, CAP, wc)
        if c == 0:
            pl.semaphore_wait(barrier, n_blk - 1 + n_band - 1)
        copies = []
        for i, k in enumerate(WINDOWS):
            copy = remote(
                keys.at[c, k], arrived.at[c, k], ka_s.at[c, i], ka_r.at[c, i],
                lax.rem(blk + MIDDLE - k + n_blk, n_blk), band,
            )
            copy.start()
            copies.append(copy)
        key_copies.append(copies)
        sent += copies
        arrived[c, MIDDLE] = keys[c, MIDDLE]

    ready("grid", "ew1")
    sproj[...] = dot(v_grid[...], v_ew[1]).astype(BF)
    ready("esnd", "eslot")

    @pl.loop(0, edges // LANES, unroll=2)
    def _(r):
        rows = pl.ds(pl.multiple_of(r * LANES, LANES), LANES)
        g_snd[rows, :] = rows_select(down_column(v_esnd[pl.ds(r, 1), :]), v_grid.shape[0])
        slot_row = v_eslot[pl.ds(r, 1), :]
        g_slot[rows, :] = rows_select(down_column(slot_row), slots)
        s_slot[:, rows] = cols_select(slot_row, slots)

    ready("bias", "gain", "ee", "ew0")
    TILE = 256

    @pl.loop(0, edges // TILE, unroll=True)
    def _(t):
        rows = pl.ds(pl.multiple_of(t * TILE, TILE), TILE)
        acc[rows, :] = (
            dot(v_ee[rows, :], v_ew[0]) + dot(g_snd[rows, :], sproj[...]) + v_bias[1, 0:1, :]
        )

    ready("ew3")

    for c in range(NC):
        for copy in key_copies[c]:
            copy.wait_recv()

        @pl.loop(0, edges // TILE, unroll=True)
        def _(t):
            rows = pl.ds(pl.multiple_of(t * TILE, TILE), TILE)
            first = acc[rows, cols[c]] + dot(g_slot[rows, :], arrived[c].reshape(slots, wc))
            second = dot(silu(first).astype(BF), v_ew[3, cols[c], :])
            if c > 0:
                second = second + opart[rows, :]
            if c < NC - 1:
                opart[rows, :] = second
            else:
                msg[rows, :] = norm(second + v_bias[1, 1:2, :], v_gain[1:2, :]).astype(BF)

    sum_copies = []
    for h in range(NC):
        halves = dot(s_slot[...], msg[:, cols[h]]).astype(BF)
        for c in range(h * NS // NC, (h + 1) * NS // NC):
            low = c * ws - h * wc
            ssum[c] = halves[:, low : low + ws].reshape(NEIGH, CAP, ws)
            copies = []
            for i, k in enumerate(WINDOWS):
                copy = remote(
                    ssum.at[c, k], landed.at[c, k], cs_s.at[c, i], cs_r.at[c, i],
                    lax.rem(blk + k - MIDDLE + n_blk, n_blk), band,
                )
                copy.start()
                copies.append(copy)
            sum_copies.append(copies)
            sent += copies
            landed[c, MIDDLE] = ssum[c, MIDDLE]

    for r in range(slots // LANES):
        select = cols_select(v_esn[0:1, r * LANES : (r + 1) * LANES], nodes)
        p_node[:, r * LANES : (r + 1) * LANES] = select
    ready("nw0", "nw1", "nw2", "msn", "msnd", "mrcv", "me", "pw")
    own_rows = pl.ds(pl.multiple_of(band * share, 32), share)

    def fill_base():
        base_mid[...] = dot(v_mesh[own_rows, :], v_nw[0]) + v_bias[2, 0:1, :]

    def fill_send():
        for r in range(v_msn.shape[1] // LANES):
            column = down_column(v_msn[0:1, r * LANES : (r + 1) * LANES])
            g_send[r * LANES : (r + 1) * LANES, :] = rows_select(column, nodes)

    def fill_edges(part, parts):
        count = medges // LANES // parts

        @pl.loop(part * count, (part + 1) * count, unroll=2)
        def _(r):
            rows = pl.ds(pl.multiple_of(r * LANES, LANES), LANES)
            acc2[rows, :] = dot(v_me[rows, :], v_pw[0]) + v_bias[3, 0:1, :]
            g_msnd[rows, :] = rows_select(down_column(v_msnd[pl.ds(r, 1), :]), slots)

    fills = [fill_base, fill_send, lambda: fill_edges(0, 2), lambda: fill_edges(1, 2)]

    def toward(c):
        return (left, right) if c == 0 else (right, left)

    def scatter_start(c, part, far, near, sem_s, sem_r):
        first, other = toward(c)
        far_copy = remote(part.at[c, across], far.at[c], sem_s.at[c, 0], sem_r.at[c, 0], blk, first)
        near_copy = remote(part.at[c, other], near.at[c], sem_s.at[c, 1], sem_r.at[c, 1], blk, other)
        far_copy.start()
        near_copy.start()
        return far_copy, near_copy

    def scatter_relay(c, far_copy, part, far, relay, relayed, sem_s, sem_r):
        first, _ = toward(c)
        far_copy.wait_recv()
        relay[c] = (far[c].astype(F32) + part[c, first].astype(F32)).astype(BF)
        copy = remote(relay.at[c], relayed.at[c], sem_s.at[c, 2], sem_r.at[c, 2], blk, first)
        copy.start()
        return copy

    pieces = []
    for c in range(NS):
        for copy in sum_copies[c]:
            copy.wait_recv()
        sums = dot(p_node[...], landed[c].reshape(slots, ws)).astype(BF)
        part[c] = sums.reshape(n_band, share, ws)
        copies = []
        for i, peer in enumerate((right, left, across)):
            copy = remote(part.at[c, peer], came.at[c, i], rs_s.at[c, i], rs_r.at[c, i], blk, peer)
            copy.start()
            copies.append(copy)
        pieces.append(copies)
        sent += copies
        if c < NS - 1:
            fills[c]()

    first = base_mid[...]
    for c in range(NS):
        total = part[c, band].astype(F32)
        for i, copy in enumerate(pieces[c]):
            copy.wait_recv()
            total = total + came[c, i].astype(F32)
        first = first + dot(total.astype(BF), v_nw[1, c * ws : (c + 1) * ws, :])
    tail = norm(dot(silu(first).astype(BF), v_nw[2]) + v_bias[2, 1:2, :], v_gain[2:3, :])
    own_mid = (v_mesh[own_rows, :].astype(F32) + tail).astype(BF)
    mid[band] = own_mid

    gathers = {}

    def spread(m, hop):
        first_peer, other_peer = toward(m % 2)
        owner = other_peer if hop == 2 else band
        block = mid.at[owner, :, m * wm : (m + 1) * wm]
        gathers[m, hop] = remote(
            block, block, ag_s.at[m, hop], ag_r.at[m, hop], blk, other_peer if hop == 1 else first_peer
        )
        gathers[m, hop].start()

    def spread_own(half):
        for hop in range(2):
            for m in half:
                spread(m, hop)

    def spread_on(half):
        for m in half:
            gathers[m, 0].wait_recv()
            spread(m, 2)

    def pick(h, half):
        for m in half:
            gathers[m, 1].wait_recv()
            gathers[m, 2].wait_recv()
        picked = dot(g_send[...], mid[:, :, cols[h]].reshape(nodes, wc))
        srows[h] = picked.reshape(srows.shape[1:]).astype(BF)

    def to_everyone(h):
        @pl.loop(0, n_blk - 1)
        def _(i):
            step = (i + 1) // 2
            r = n_blk // 2 + step * (1 - 2 * lax.rem(i, 2))
            to = lax.rem(blk + r, n_blk)
            remote(srows.at[h, to], arr.at[h, blk], aa_s.at[h], aa_r.at[h], to, band).start()

        arr[h, blk] = srows[h, blk]

    halves = [range(h * NM // NC, (h + 1) * NM // NC) for h in range(NC)]
    spread_own(halves[0])
    spread_on(halves[0])
    spread_own(halves[1])
    pick(0, halves[0])
    spread_on(halves[1])
    to_everyone(0)
    pick(1, halves[1])
    to_everyone(1)
    fills[NS - 1]()
    sent += list(gathers.values())

    tkeys[...] = dot(mid[...].reshape(nodes, width), v_pw[2]).astype(BF)

    @pl.loop(0, medges // LANES, unroll=2)
    def _(r):
        rows = pl.ds(pl.multiple_of(r * LANES, LANES), LANES)
        receiver_row = v_mrcv[pl.ds(r, 1), :]
        select = rows_select(down_column(receiver_row), nodes)
        acc2[rows, :] = acc2[rows, :] + dot(select, tkeys[...])
        r_rcv[:, rows] = cols_select(receiver_row, nodes)

    ready("gw")

    @pl.loop(0, v_grid.shape[0] // TILE, unroll=True)
    def _(t):
        rows = pl.ds(pl.multiple_of(t * TILE, TILE), TILE)
        first = dot(v_grid[rows, :], v_gw[0]) + v_bias[0, 0:1, :]
        tail = norm(dot(silu(first).astype(BF), v_gw[1]) + v_bias[0, 1:2, :], v_gain[0:1, :])
        v_go[rows, :] = (v_grid[rows, :].astype(F32) + tail).astype(BF)

    ready("fw")
    base_fin[...] = dot(mid[band], v_fw[0]) + v_bias[4, 0:1, :]

    blocks = pl.ds(0, n_blk - 1)
    everyone = [
        remote(srows.at[h, blocks], arr.at[h, blocks], aa_s.at[h], aa_r.at[h], blk, band)
        for h in range(NC)
    ]
    requested = None
    for h in range(NC):
        everyone[h].wait_recv()
        raw = arr[h].astype(F32).reshape(arr2.shape[0], wc).astype(BF)
        term = dot(raw, v_pw[1, cols[h], :])
        if h < NC - 1:
            opart[0 : arr2.shape[0], :] = term if requested is None else opart[0 : arr2.shape[0], :] + term
            requested = opart
        else:
            arr2[...] = (opart[0 : arr2.shape[0], :] + term).astype(BF)

    @pl.loop(0, medges // TILE, unroll=True)
    def _(t):
        rows = pl.ds(pl.multiple_of(t * TILE, TILE), TILE)
        first = acc2[rows, :] + dot(g_msnd[rows, :], arr2[...])
        second = dot(silu(first).astype(BF), v_pw[3]) + v_bias[3, 1:2, :]
        msg[rows, :] = norm(second, v_gain[3:4, :]).astype(BF)

    scatters = []
    for c in range(NC):
        sums = dot(r_rcv[...], msg[:, cols[c]]).astype(BF)
        part2[c] = sums.reshape(n_band, share, wc)
        scatters.append(scatter_start(c, part2, far2, near2, rt_s, rt_r))
    relays = []
    for c in range(NC):
        relays.append(scatter_relay(c, scatters[c][0], part2, far2, relay2, relayed2, rt_s, rt_r))
        sent += [*scatters[c], relays[c]]
    first = base_fin[...]
    for c in range(NC):
        scatters[c][1].wait_recv()
        relays[c].wait_recv()
        total = part2[c, band].astype(F32) + near2[c].astype(F32) + relayed2[c].astype(F32)
        first = first + dot(total.astype(BF), v_fw[1, cols[c], :])
    tail = norm(dot(silu(first).astype(BF), v_fw[2]) + v_bias[4, 1:2, :], v_gain[4:5, :])
    for c in range(NC):
        v_mo[:, cols[c]] = (mid[band, :, cols[c]].astype(F32) + tail[:, cols[c]]).astype(BF)
    for copy in sent:
        copy.wait_send()
    for copy in everyone:
        copy.wait_send()


def handed_on(v_grid, v_mesh, grid_out, mesh_out, sem):
    copies = [
        pltpu.make_async_copy(v_mesh, mesh_out, sem.at[0]),
        pltpu.make_async_copy(v_grid, grid_out, sem.at[1]),
    ]
    for copy in copies:
        copy.start()
    for copy in copies:
        copy.wait()


def per_device(n_blk, n_band, *args):
    (grid_nodes, enc_edges, enc_sender, enc_slot, enc_slot_node, mesh_nodes, mesh_edges,
     mesh_sender, mesh_receiver, mesh_send_node, *params) = args

    def folded(index):
        return index.reshape(-1, LANES)

    args = (grid_nodes, enc_edges, folded(enc_sender), folded(enc_slot), enc_slot_node, mesh_nodes,
            mesh_edges, folded(mesh_sender), folded(mesh_receiver), mesh_send_node, *params)
    width = mesh_nodes.shape[1]
    wc = width // NC
    nodes = mesh_nodes.shape[0]
    share = nodes // n_band
    grid_rows = grid_nodes.shape[0]
    edges, medges = enc_edges.shape[0], mesh_edges.shape[0]
    slots = NEIGH * CAP
    requests = mesh_send_node.shape[1]
    vm = pltpu.VMEM
    dma = pltpu.SemaphoreType.DMA
    scratch = [vm(a.shape, a.dtype) for a in args]
    window = (NC, NEIGH, CAP, wc)
    shares, piece = (NC, n_band, share, wc), (NC, share, wc)
    boxes = (NC, n_blk, requests // n_blk, wc)
    ws = width // NS
    scratch += [vm(window, BF)] * 2 + [vm((NS, NEIGH, CAP, ws), BF)] * 2
    scratch += [vm((NS, n_band, share, ws), BF), vm((NS, n_band - 1, share, ws), BF)]
    scratch += [vm((n_band, share, width), BF), vm(boxes, BF), vm(boxes, BF), vm((requests, width), BF)]
    scratch += [vm(shares, BF)] + [vm(piece, BF)] * 4
    scratch += [
        vm((slots, nodes), BF), vm((edges, slots), BF), vm((slots, edges), BF),
        vm((edges, grid_rows), BF), vm((nodes, slots), BF), vm((requests, nodes), BF),
        vm((medges, requests), BF), vm((8, LANES), BF), vm((nodes, medges), BF),
    ]
    scratch += [
        vm((grid_rows, width), BF), vm((edges, width), F32), vm((medges, width), F32),
        vm((edges, width), F32), vm((max(edges, medges), width), BF), vm((share, width), F32),
        vm((share, width), F32), vm((slots, width), BF), vm((nodes, width), BF),
    ]
    near = len(WINDOWS)
    scratch += [dma((24,))]
    scratch += [dma((NC, near))] * 2 + [dma((NS, near))] * 2
    scratch += [dma((NS, 3))] * 2 + [dma((NM, 3))] * 2
    scratch += [dma((NC,))] * 2 + [dma((NC, 3))] * 2
    anywhere = pl.BlockSpec(memory_space=pl.ANY)
    on_chip = pl.BlockSpec(memory_space=pltpu.VMEM)
    results = pl.pallas_call(
        kernel,
        out_shape=(vm((grid_rows, width), BF), vm((share, width), BF)),
        in_specs=[anywhere] * len(args),
        out_specs=(on_chip, on_chip),
        scratch_shapes=scratch,
        compiler_params=pltpu.CompilerParams(
            collective_id=0, has_side_effects=True, vmem_limit_bytes=60 * 1024 * 1024
        ),
        name="encoder_processor",
    )(*args)
    return pl.pallas_call(
        handed_on,
        out_shape=tuple(jax.ShapeDtypeStruct(r.shape, r.dtype) for r in results),
        in_specs=[anywhere] * 2,
        out_specs=(anywhere, anywhere),
        scratch_shapes=[dma((2,))],
        name="handed_on",
    )(*[pltpu.with_memory_space_constraint(r, pltpu.VMEM) for r in results])


def solution(mesh):
    rows = P(("blk", "band"), None)
    flat = P(("blk", "band"))
    in_specs = (rows, rows, flat, flat, rows, P("blk", None), rows, flat, flat, rows) + (P(),) * 7
    n_blk, n_band = mesh.shape["blk"], mesh.shape["band"]

    def step(*args):
        return per_device(n_blk, n_band, *args)

    return jax.shard_map(
        step, mesh=mesh, in_specs=in_specs, out_specs=(rows, rows), check_vma=False
    )
```

```python
import jax
import jax.numpy as jnp
from jax import lax
from jax.experimental import pallas as pl
from jax.experimental.pallas import tpu as pltpu
from jax.sharding import PartitionSpec as P

NEIGH = 8
CAP = 64
MIDDLE = NEIGH // 2
WINDOWS = [0, 1, 7, 2, 6, 5, 3]
NC = 2
NS = 4
NM = 4
MESH = pl.DeviceIdType.MESH
BF = jnp.bfloat16
F32 = jnp.float32
LANES = 128


def dot(a, b):
    return jnp.dot(a, b, preferred_element_type=F32)


def silu(v):
    half = 0.5 * v
    return half + half * jnp.tanh(half)


def norm(values, gain_row):
    center = values - jnp.mean(values, axis=-1, keepdims=True)
    spread = jnp.mean(center * center, axis=-1, keepdims=True)
    return center * lax.rsqrt(spread + 1e-05) * gain_row


def one_hot(flags):
    return jnp.where(flags, 1.0, 0.0).astype(BF)


def down_column(row):
    return jnp.transpose(jnp.broadcast_to(row, (LANES, LANES)))


def rows_select(column, width, start=0):
    lane = lax.broadcasted_iota(jnp.int32, (LANES, LANES), 1)
    return jnp.concatenate(
        [one_hot(column == lane + (start + j)) for j in range(0, width, LANES)], axis=1
    )


def cols_select(row, height):
    return one_hot(lax.broadcasted_iota(jnp.int32, (height, LANES), 0) == row)


def kernel(
    grid_nodes, enc_edges, enc_sender, enc_slot, enc_slot_node, mesh_nodes, mesh_edges,
    mesh_sender, mesh_receiver, mesh_send_node, grid_w, enc_w, node_w, proc_w, final_w,
    biases, gains,
    v_go, v_mo,
    v_grid, v_ee, v_esnd, v_eslot, v_esn, v_mesh, v_me, v_msnd, v_mrcv, v_msn,
    v_gw, v_ew, v_nw, v_pw, v_fw, v_bias, v_gain,
    keys, arrived, ssum, landed, part, came, mid, srows, arr, arr2,
    part2, far2, near2, relay2, relayed2,
    g_key, g_slot, s_slot, g_snd, p_node, g_send, g_msnd, g_rcv, r_rcv,
    sproj, acc, acc2, opart, msg, base_mid, base_fin, gsel, tkeys,
    load_sem, ka_s, ka_r, cs_s, cs_r, rs_s, rs_r, ag_s, ag_r, aa_s, aa_r, rt_s, rt_r,
):
    n_blk = lax.axis_size("blk")
    n_band = lax.axis_size("band")
    blk = lax.axis_index("blk")
    band = lax.axis_index("band")
    left = lax.rem(band + n_band - 1, n_band)
    right = lax.rem(band + 1, n_band)
    across = lax.rem(band + 2, n_band)
    width = v_mesh.shape[1]
    wc = width // NC
    ws = width // NS
    wm = width // NM
    nodes = v_mesh.shape[0]
    share = nodes // n_band
    slots = NEIGH * CAP
    edges = v_ee.shape[0]
    medges = v_me.shape[0]
    cols = [slice(c * wc, (c + 1) * wc) for c in range(NC)]

    loads = {}

    def load(name, src, dst):
        copy = pltpu.make_async_copy(src, dst, load_sem.at[len(loads)])
        copy.start()
        loads[name] = copy

    def ready(*names):
        for name in names:
            loads[name].wait()

    load("esn", enc_slot_node, v_esn)
    load("mesh", mesh_nodes, v_mesh)
    load("ew2", enc_w.at[2], v_ew.at[2])

    barrier = pltpu.get_barrier_semaphore()

    @pl.loop(1, n_blk)
    def _(r):
        pl.semaphore_signal(
            barrier, inc=1, device_id=(lax.rem(blk + r, n_blk), band), device_id_type=MESH
        )

    for peer in (left, right, across):
        pl.semaphore_signal(barrier, inc=1, device_id=(blk, peer), device_id_type=MESH)

    load("grid", grid_nodes, v_grid)
    load("ew1", enc_w.at[1], v_ew.at[1])
    load("esnd", enc_sender, v_esnd)
    load("eslot", enc_slot, v_eslot)
    load("bias", biases, v_bias)
    load("gain", gains, v_gain)
    load("ee", enc_edges, v_ee)
    load("ew0", enc_w.at[0], v_ew.at[0])
    load("ew3", enc_w.at[3], v_ew.at[3])
    load("nw0", node_w.at[0], v_nw.at[0])
    load("nw1", node_w.at[1], v_nw.at[1])
    load("nw2", node_w.at[2], v_nw.at[2])
    load("msn", mesh_send_node, v_msn)
    load("msnd", mesh_sender, v_msnd)
    load("mrcv", mesh_receiver, v_mrcv)
    load("me", mesh_edges, v_me)
    load("pw", proc_w, v_pw)
    load("gw", grid_w, v_gw)
    load("fw", final_w, v_fw)

    def remote(src, dst, send, recv, to_blk, to_band):
        return pltpu.make_async_remote_copy(
            src_ref=src, dst_ref=dst, send_sem=send, recv_sem=recv,
            device_id=(to_blk, to_band), device_id_type=MESH,
        )

    sent = []

    ready("esn")
    for r in range(slots // LANES):
        column = down_column(v_esn[0:1, r * LANES : (r + 1) * LANES])
        g_key[r * LANES : (r + 1) * LANES, :] = rows_select(column, nodes)
    ready("mesh", "ew2")
    gsel[...] = dot(g_key[...], v_mesh[...]).astype(BF)
    key_copies = []
    for c in range(NC):
        projected = dot(gsel[...], v_ew[2, :, cols[c]]).astype(BF)
        keys[c] = projected.reshape(NEIGH, CAP, wc)
        if c == 0:
            pl.semaphore_wait(barrier, n_blk - 1 + n_band - 1)
        copies = []
        for i, k in enumerate(WINDOWS):
            copy = remote(
                keys.at[c, k], arrived.at[c, k], ka_s.at[c, i], ka_r.at[c, i],
                lax.rem(blk + MIDDLE - k + n_blk, n_blk), band,
            )
            copy.start()
            copies.append(copy)
        key_copies.append(copies)
        sent += copies
        arrived[c, MIDDLE] = keys[c, MIDDLE]

    ready("grid", "ew1")
    sproj[...] = dot(v_grid[...], v_ew[1]).astype(BF)
    ready("esnd", "eslot")

    @pl.loop(0, edges // LANES, unroll=2)
    def _(r):
        rows = pl.ds(pl.multiple_of(r * LANES, LANES), LANES)
        g_snd[rows, :] = rows_select(down_column(v_esnd[pl.ds(r, 1), :]), v_grid.shape[0])
        slot_row = v_eslot[pl.ds(r, 1), :]
        g_slot[rows, :] = rows_select(down_column(slot_row), slots)
        s_slot[:, rows] = cols_select(slot_row, slots)

    ready("bias", "gain", "ee", "ew0")
    TILE = 256

    @pl.loop(0, edges // TILE, unroll=True)
    def _(t):
        rows = pl.ds(pl.multiple_of(t * TILE, TILE), TILE)
        acc[rows, :] = (
            dot(v_ee[rows, :], v_ew[0]) + dot(g_snd[rows, :], sproj[...]) + v_bias[1, 0:1, :]
        )

    ready("ew3")

    for c in range(NC):
        for copy in key_copies[c]:
            copy.wait_recv()

        @pl.loop(0, edges // TILE, unroll=True)
        def _(t):
            rows = pl.ds(pl.multiple_of(t * TILE, TILE), TILE)
            first = acc[rows, cols[c]] + dot(g_slot[rows, :], arrived[c].reshape(slots, wc))
            second = dot(silu(first).astype(BF), v_ew[3, cols[c], :])
            if c > 0:
                second = second + opart[rows, :]
            if c < NC - 1:
                opart[rows, :] = second
            else:
                msg[rows, :] = norm(second + v_bias[1, 1:2, :], v_gain[1:2, :]).astype(BF)

    sum_copies = []
    for h in range(NC):
        halves = dot(s_slot[...], msg[:, cols[h]]).astype(BF)
        for c in range(h * NS // NC, (h + 1) * NS // NC):
            low = c * ws - h * wc
            ssum[c] = halves[:, low : low + ws].reshape(NEIGH, CAP, ws)
            copies = []
            for i, k in enumerate(WINDOWS):
                copy = remote(
                    ssum.at[c, k], landed.at[c, k], cs_s.at[c, i], cs_r.at[c, i],
                    lax.rem(blk + k - MIDDLE + n_blk, n_blk), band,
                )
                copy.start()
                copies.append(copy)
            sum_copies.append(copies)
            sent += copies
            landed[c, MIDDLE] = ssum[c, MIDDLE]

    for r in range(slots // LANES):
        select = cols_select(v_esn[0:1, r * LANES : (r + 1) * LANES], nodes)
        p_node[:, r * LANES : (r + 1) * LANES] = select
    ready("nw0", "nw1", "nw2", "msn", "msnd", "mrcv", "me", "pw")
    own_rows = pl.ds(pl.multiple_of(band * share, 32), share)

    def fill_base():
        base_mid[...] = dot(v_mesh[own_rows, :], v_nw[0]) + v_bias[2, 0:1, :]

    def fill_send():
        for r in range(v_msn.shape[1] // LANES):
            column = down_column(v_msn[0:1, r * LANES : (r + 1) * LANES])
            g_send[r * LANES : (r + 1) * LANES, :] = rows_select(column, nodes)

    def fill_edges(part, parts):
        count = medges // LANES // parts

        @pl.loop(part * count, (part + 1) * count, unroll=2)
        def _(r):
            rows = pl.ds(pl.multiple_of(r * LANES, LANES), LANES)
            acc2[rows, :] = dot(v_me[rows, :], v_pw[0]) + v_bias[3, 0:1, :]
            g_msnd[rows, :] = rows_select(down_column(v_msnd[pl.ds(r, 1), :]), slots)

    fill_base()
    fill_send()

    def toward(c):
        return (left, right) if c == 0 else (right, left)

    def scatter_start(c, part, far, near, sem_s, sem_r):
        first, other = toward(c)
        far_copy = remote(part.at[c, across], far.at[c], sem_s.at[c, 0], sem_r.at[c, 0], blk, first)
        near_copy = remote(part.at[c, other], near.at[c], sem_s.at[c, 1], sem_r.at[c, 1], blk, other)
        far_copy.start()
        return far_copy, near_copy

    def scatter_relay(c, far_copy, part, far, relay, relayed, sem_s, sem_r):
        first, _ = toward(c)
        far_copy.wait_recv()
        relay[c] = (far[c].astype(F32) + part[c, first].astype(F32)).astype(BF)
        copy = remote(relay.at[c], relayed.at[c], sem_s.at[c, 2], sem_r.at[c, 2], blk, first)
        copy.start()
        return copy

    pieces = []
    for c in range(NS):
        for copy in sum_copies[c]:
            copy.wait_recv()
        sums = dot(p_node[...], landed[c].reshape(slots, ws)).astype(BF)
        part[c] = sums.reshape(n_band, share, ws)
        copies = []
        for i, peer in enumerate((right, left, across)):
            copy = remote(part.at[c, peer], came.at[c, i], rs_s.at[c, i], rs_r.at[c, i], blk, peer)
            copy.start()
            copies.append(copy)
        pieces.append(copies)
        sent += copies

    first = base_mid[...]
    for c in range(NS):
        total = part[c, band].astype(F32)
        for i, copy in enumerate(pieces[c]):
            copy.wait_recv()
            total = total + came[c, i].astype(F32)
        first = first + dot(total.astype(BF), v_nw[1, c * ws : (c + 1) * ws, :])
    tail = norm(dot(silu(first).astype(BF), v_nw[2]) + v_bias[2, 1:2, :], v_gain[2:3, :])
    own_mid = (v_mesh[own_rows, :].astype(F32) + tail).astype(BF)
    mid[band] = own_mid

    gathers = {}

    def spread(m, hop):
        first_peer, other_peer = toward(m % 2)
        owner = other_peer if hop == 2 else band
        block = mid.at[owner, :, m * wm : (m + 1) * wm]
        gathers[m, hop] = remote(
            block, block, ag_s.at[m, hop], ag_r.at[m, hop], blk, other_peer if hop == 1 else first_peer
        )
        gathers[m, hop].start()

    def spread_own(half):
        for hop in range(2):
            for m in half:
                spread(m, hop)

    def spread_on(half):
        for m in half:
            gathers[m, 0].wait_recv()
            spread(m, 2)

    def pick(h, half):
        for m in half:
            gathers[m, 1].wait_recv()
            gathers[m, 2].wait_recv()
        picked = dot(g_send[...], mid[:, :, cols[h]].reshape(nodes, wc))
        srows[h] = picked.reshape(srows.shape[1:]).astype(BF)

    def to_everyone(h):
        @pl.loop(0, n_blk - 1)
        def _(i):
            step = (i + 1) // 2
            r = n_blk // 2 + step * (1 - 2 * lax.rem(i, 2))
            to = lax.rem(blk + r, n_blk)
            remote(srows.at[h, to], arr.at[h, blk], aa_s.at[h], aa_r.at[h], to, band).start()

        arr[h, blk] = srows[h, blk]

    halves = [range(h * NM // NC, (h + 1) * NM // NC) for h in range(NC)]
    spread_own(halves[0])
    spread_on(halves[0])
    spread_own(halves[1])
    pick(0, halves[0])
    spread_on(halves[1])
    to_everyone(0)
    pick(1, halves[1])
    to_everyone(1)
    fill_edges(0, 1)
    sent += list(gathers.values())

    tkeys[...] = dot(mid[...].reshape(nodes, width), v_pw[2]).astype(BF)

    @pl.loop(0, medges // LANES, unroll=2)
    def _(r):
        rows = pl.ds(pl.multiple_of(r * LANES, LANES), LANES)
        receiver_row = v_mrcv[pl.ds(r, 1), :]
        select = rows_select(down_column(receiver_row), nodes)
        acc2[rows, :] = acc2[rows, :] + dot(select, tkeys[...])
        r_rcv[:, rows] = cols_select(receiver_row, nodes)

    ready("gw")

    @pl.loop(0, v_grid.shape[0] // TILE, unroll=True)
    def _(t):
        rows = pl.ds(pl.multiple_of(t * TILE, TILE), TILE)
        first = dot(v_grid[rows, :], v_gw[0]) + v_bias[0, 0:1, :]
        tail = norm(dot(silu(first).astype(BF), v_gw[1]) + v_bias[0, 1:2, :], v_gain[0:1, :])
        v_go[rows, :] = (v_grid[rows, :].astype(F32) + tail).astype(BF)

    ready("fw")
    base_fin[...] = dot(mid[band], v_fw[0]) + v_bias[4, 0:1, :]

    blocks = pl.ds(0, n_blk - 1)
    everyone = [
        remote(srows.at[h, blocks], arr.at[h, blocks], aa_s.at[h], aa_r.at[h], blk, band)
        for h in range(NC)
    ]
    requested = None
    for h in range(NC):
        everyone[h].wait_recv()
        raw = arr[h].astype(F32).reshape(arr2.shape[0], wc).astype(BF)
        term = dot(raw, v_pw[1, cols[h], :])
        if h < NC - 1:
            opart[0 : arr2.shape[0], :] = term if requested is None else opart[0 : arr2.shape[0], :] + term
            requested = opart
        else:
            arr2[...] = (opart[0 : arr2.shape[0], :] + term).astype(BF)

    @pl.loop(0, medges // TILE, unroll=True)
    def _(t):
        rows = pl.ds(pl.multiple_of(t * TILE, TILE), TILE)
        first = acc2[rows, :] + dot(g_msnd[rows, :], arr2[...])
        second = dot(silu(first).astype(BF), v_pw[3]) + v_bias[3, 1:2, :]
        msg[rows, :] = norm(second, v_gain[3:4, :]).astype(BF)

    scatters = []
    for c in range(NC):
        sums = dot(r_rcv[...], msg[:, cols[c]]).astype(BF)
        part2[c] = sums.reshape(n_band, share, wc)
        scatters.append(scatter_start(c, part2, far2, near2, rt_s, rt_r))
    for far_copy, near_copy in scatters:
        far_copy.wait_send()
        near_copy.start()
    relays = []
    for c in range(NC):
        relays.append(scatter_relay(c, scatters[c][0], part2, far2, relay2, relayed2, rt_s, rt_r))
        sent += [scatters[c][1], relays[c]]
    first = base_fin[...]
    for c in range(NC):
        scatters[c][1].wait_recv()
        relays[c].wait_recv()
        total = part2[c, band].astype(F32) + near2[c].astype(F32) + relayed2[c].astype(F32)
        first = first + dot(total.astype(BF), v_fw[1, cols[c], :])
    tail = norm(dot(silu(first).astype(BF), v_fw[2]) + v_bias[4, 1:2, :], v_gain[4:5, :])
    for c in range(NC):
        v_mo[:, cols[c]] = (mid[band, :, cols[c]].astype(F32) + tail[:, cols[c]]).astype(BF)
    for copy in sent:
        copy.wait_send()
    for copy in everyone:
        copy.wait_send()


def handed_on(v_grid, v_mesh, grid_out, mesh_out, sem):
    copies = [
        pltpu.make_async_copy(v_mesh, mesh_out, sem.at[0]),
        pltpu.make_async_copy(v_grid, grid_out, sem.at[1]),
    ]
    for copy in copies:
        copy.start()
    for copy in copies:
        copy.wait()


def per_device(n_blk, n_band, *args):
    (grid_nodes, enc_edges, enc_sender, enc_slot, enc_slot_node, mesh_nodes, mesh_edges,
     mesh_sender, mesh_receiver, mesh_send_node, *params) = args

    def folded(index):
        return index.reshape(-1, LANES)

    args = (grid_nodes, enc_edges, folded(enc_sender), folded(enc_slot), enc_slot_node, mesh_nodes,
            mesh_edges, folded(mesh_sender), folded(mesh_receiver), mesh_send_node, *params)
    width = mesh_nodes.shape[1]
    wc = width // NC
    nodes = mesh_nodes.shape[0]
    share = nodes // n_band
    grid_rows = grid_nodes.shape[0]
    edges, medges = enc_edges.shape[0], mesh_edges.shape[0]
    slots = NEIGH * CAP
    requests = mesh_send_node.shape[1]
    vm = pltpu.VMEM
    dma = pltpu.SemaphoreType.DMA
    scratch = [vm(a.shape, a.dtype) for a in args]
    window = (NC, NEIGH, CAP, wc)
    shares, piece = (NC, n_band, share, wc), (NC, share, wc)
    boxes = (NC, n_blk, requests // n_blk, wc)
    ws = width // NS
    scratch += [vm(window, BF)] * 2 + [vm((NS, NEIGH, CAP, ws), BF)] * 2
    scratch += [vm((NS, n_band, share, ws), BF), vm((NS, n_band - 1, share, ws), BF)]
    scratch += [vm((n_band, share, width), BF), vm(boxes, BF), vm(boxes, BF), vm((requests, width), BF)]
    scratch += [vm(shares, BF)] + [vm(piece, BF)] * 4
    scratch += [
        vm((slots, nodes), BF), vm((edges, slots), BF), vm((slots, edges), BF),
        vm((edges, grid_rows), BF), vm((nodes, slots), BF), vm((requests, nodes), BF),
        vm((medges, requests), BF), vm((8, LANES), BF), vm((nodes, medges), BF),
    ]
    scratch += [
        vm((grid_rows, width), BF), vm((edges, width), F32), vm((medges, width), F32),
        vm((edges, width), F32), vm((max(edges, medges), width), BF), vm((share, width), F32),
        vm((share, width), F32), vm((slots, width), BF), vm((nodes, width), BF),
    ]
    near = len(WINDOWS)
    scratch += [dma((24,))]
    scratch += [dma((NC, near))] * 2 + [dma((NS, near))] * 2
    scratch += [dma((NS, 3))] * 2 + [dma((NM, 3))] * 2
    scratch += [dma((NC,))] * 2 + [dma((NC, 3))] * 2
    anywhere = pl.BlockSpec(memory_space=pl.ANY)
    on_chip = pl.BlockSpec(memory_space=pltpu.VMEM)
    results = pl.pallas_call(
        kernel,
        out_shape=(vm((grid_rows, width), BF), vm((share, width), BF)),
        in_specs=[anywhere] * len(args),
        out_specs=(on_chip, on_chip),
        scratch_shapes=scratch,
        compiler_params=pltpu.CompilerParams(
            collective_id=0, has_side_effects=True, vmem_limit_bytes=60 * 1024 * 1024
        ),
        name="encoder_processor",
    )(*args)
    return pl.pallas_call(
        handed_on,
        out_shape=tuple(jax.ShapeDtypeStruct(r.shape, r.dtype) for r in results),
        in_specs=[anywhere] * 2,
        out_specs=(anywhere, anywhere),
        scratch_shapes=[dma((2,))],
        name="handed_on",
    )(*[pltpu.with_memory_space_constraint(r, pltpu.VMEM) for r in results])


def solution(mesh):
    rows = P(("blk", "band"), None)
    flat = P(("blk", "band"))
    in_specs = (rows, rows, flat, flat, rows, P("blk", None), rows, flat, flat, rows) + (P(),) * 7
    n_blk, n_band = mesh.shape["blk"], mesh.shape["band"]

    def step(*args):
        return per_device(n_blk, n_band, *args)

    return jax.shard_map(
        step, mesh=mesh, in_specs=in_specs, out_specs=(rows, rows), check_vma=False
    )
```

```python
import jax
import jax.numpy as jnp
from jax import lax
from jax.experimental import pallas as pl
from jax.experimental.pallas import tpu as pltpu
from jax.sharding import PartitionSpec as P

NEIGH = 8
CAP = 64
MIDDLE = NEIGH // 2
WINDOWS = [0, 1, 7, 2, 6, 5, 3]
NC = 2
NS = 4
NM = 4
MESH = pl.DeviceIdType.MESH
BF = jnp.bfloat16
F32 = jnp.float32
LANES = 128


def dot(a, b):
    return jnp.dot(a, b, preferred_element_type=F32)


def silu(v):
    half = 0.5 * v
    return half + half * jnp.tanh(half)


def norm(values, gain_row):
    center = values - jnp.mean(values, axis=-1, keepdims=True)
    spread = jnp.mean(center * center, axis=-1, keepdims=True)
    return center * lax.rsqrt(spread + 1e-05) * gain_row


def one_hot(flags):
    return jnp.where(flags, 1.0, 0.0).astype(BF)


def down_column(row):
    return jnp.transpose(jnp.broadcast_to(row, (LANES, LANES)))


def rows_select(column, width, start=0):
    lane = lax.broadcasted_iota(jnp.int32, (LANES, LANES), 1)
    return jnp.concatenate(
        [one_hot(column == lane + (start + j)) for j in range(0, width, LANES)], axis=1
    )


def cols_select(row, height):
    return one_hot(lax.broadcasted_iota(jnp.int32, (height, LANES), 0) == row)


def kernel(
    grid_nodes, enc_edges, enc_sender, enc_slot, enc_slot_node, mesh_nodes, mesh_edges,
    mesh_sender, mesh_receiver, mesh_send_node, grid_w, enc_w, node_w, proc_w, final_w,
    biases, gains,
    v_go, v_mo,
    v_grid, v_ee, v_esnd, v_eslot, v_esn, v_mesh, v_me, v_msnd, v_mrcv, v_msn,
    v_gw, v_ew, v_nw, v_pw, v_fw, v_bias, v_gain,
    keys, arrived, ssum, landed, part, came, mid, srows, arr, arr2,
    part2, far2, near2, relay2, relayed2,
    g_key, g_slot, s_slot, g_snd, p_node, g_send, g_msnd, g_rcv, r_rcv,
    sproj, acc, acc2, opart, msg, base_mid, base_fin, gsel, tkeys,
    load_sem, ka_s, ka_r, cs_s, cs_r, rs_s, rs_r, ag_s, ag_r, aa_s, aa_r, rt_s, rt_r,
):
    n_blk = lax.axis_size("blk")
    n_band = lax.axis_size("band")
    blk = lax.axis_index("blk")
    band = lax.axis_index("band")
    left = lax.rem(band + n_band - 1, n_band)
    right = lax.rem(band + 1, n_band)
    across = lax.rem(band + 2, n_band)
    width = v_mesh.shape[1]
    wc = width // NC
    ws = width // NS
    wm = width // NM
    nodes = v_mesh.shape[0]
    share = nodes // n_band
    slots = NEIGH * CAP
    edges = v_ee.shape[0]
    medges = v_me.shape[0]
    cols = [slice(c * wc, (c + 1) * wc) for c in range(NC)]

    loads = {}

    def load(name, src, dst):
        copy = pltpu.make_async_copy(src, dst, load_sem.at[len(loads)])
        copy.start()
        loads[name] = copy

    def ready(*names):
        for name in names:
            loads[name].wait()

    load("esn", enc_slot_node, v_esn)
    load("mesh", mesh_nodes, v_mesh)
    load("ew2", enc_w.at[2], v_ew.at[2])

    barrier = pltpu.get_barrier_semaphore()

    @pl.loop(1, n_blk)
    def _(r):
        pl.semaphore_signal(
            barrier, inc=1, device_id=(lax.rem(blk + r, n_blk), band), device_id_type=MESH
        )

    for peer in (left, right, across):
        pl.semaphore_signal(barrier, inc=1, device_id=(blk, peer), device_id_type=MESH)

    load("grid", grid_nodes, v_grid)
    load("ew1", enc_w.at[1], v_ew.at[1])
    load("esnd", enc_sender, v_esnd)
    load("eslot", enc_slot, v_eslot)
    load("bias", biases, v_bias)
    load("gain", gains, v_gain)
    load("ee", enc_edges, v_ee)
    load("ew0", enc_w.at[0], v_ew.at[0])
    load("ew3", enc_w.at[3], v_ew.at[3])
    load("nw0", node_w.at[0], v_nw.at[0])
    load("nw1", node_w.at[1], v_nw.at[1])
    load("nw2", node_w.at[2], v_nw.at[2])
    load("msn", mesh_send_node, v_msn)
    load("msnd", mesh_sender, v_msnd)
    load("mrcv", mesh_receiver, v_mrcv)
    load("me", mesh_edges, v_me)
    load("pw", proc_w, v_pw)
    load("gw", grid_w, v_gw)
    load("fw", final_w, v_fw)

    def remote(src, dst, send, recv, to_blk, to_band):
        return pltpu.make_async_remote_copy(
            src_ref=src, dst_ref=dst, send_sem=send, recv_sem=recv,
            device_id=(to_blk, to_band), device_id_type=MESH,
        )

    sent = []

    ready("esn")
    for r in range(slots // LANES):
        column = down_column(v_esn[0:1, r * LANES : (r + 1) * LANES])
        g_key[r * LANES : (r + 1) * LANES, :] = rows_select(column, nodes)
    ready("mesh", "ew2")
    gsel[...] = dot(g_key[...], v_mesh[...]).astype(BF)
    key_copies = []
    for c in range(NC):
        projected = dot(gsel[...], v_ew[2, :, cols[c]]).astype(BF)
        keys[c] = projected.reshape(NEIGH, CAP, wc)
        if c == 0:
            pl.semaphore_wait(barrier, n_blk - 1 + n_band - 1)
        copies = []
        for i, k in enumerate(WINDOWS):
            copy = remote(
                keys.at[c, k], arrived.at[c, k], ka_s.at[c, i], ka_r.at[c, i],
                lax.rem(blk + MIDDLE - k + n_blk, n_blk), band,
            )
            copy.start()
            copies.append(copy)
        key_copies.append(copies)
        sent += copies
        arrived[c, MIDDLE] = keys[c, MIDDLE]

    ready("grid", "ew1")
    sproj[...] = dot(v_grid[...], v_ew[1]).astype(BF)
    ready("esnd", "eslot")

    @pl.loop(0, edges // LANES, unroll=2)
    def _(r):
        rows = pl.ds(pl.multiple_of(r * LANES, LANES), LANES)
        g_snd[rows, :] = rows_select(down_column(v_esnd[pl.ds(r, 1), :]), v_grid.shape[0])
        slot_row = v_eslot[pl.ds(r, 1), :]
        g_slot[rows, :] = rows_select(down_column(slot_row), slots)
        s_slot[:, rows] = cols_select(slot_row, slots)

    ready("bias", "gain", "ee", "ew0")
    TILE = 256

    @pl.loop(0, edges // TILE, unroll=True)
    def _(t):
        rows = pl.ds(pl.multiple_of(t * TILE, TILE), TILE)
        acc[rows, :] = (
            dot(v_ee[rows, :], v_ew[0]) + dot(g_snd[rows, :], sproj[...]) + v_bias[1, 0:1, :]
        )

    ready("ew3")

    for c in range(NC):
        for copy in key_copies[c]:
            copy.wait_recv()

        @pl.loop(0, edges // TILE, unroll=True)
        def _(t):
            rows = pl.ds(pl.multiple_of(t * TILE, TILE), TILE)
            first = acc[rows, cols[c]] + dot(g_slot[rows, :], arrived[c].reshape(slots, wc))
            second = dot(silu(first).astype(BF), v_ew[3, cols[c], :])
            if c > 0:
                second = second + opart[rows, :]
            if c < NC - 1:
                opart[rows, :] = second
            else:
                msg[rows, :] = norm(second + v_bias[1, 1:2, :], v_gain[1:2, :]).astype(BF)

    sum_copies = []
    for h in range(NC):
        halves = dot(s_slot[...], msg[:, cols[h]]).astype(BF)
        for c in range(h * NS // NC, (h + 1) * NS // NC):
            low = c * ws - h * wc
            ssum[c] = halves[:, low : low + ws].reshape(NEIGH, CAP, ws)
            copies = []
            for i, k in enumerate(WINDOWS):
                copy = remote(
                    ssum.at[c, k], landed.at[c, k], cs_s.at[c, i], cs_r.at[c, i],
                    lax.rem(blk + k - MIDDLE + n_blk, n_blk), band,
                )
                copy.start()
                copies.append(copy)
            sum_copies.append(copies)
            sent += copies
            landed[c, MIDDLE] = ssum[c, MIDDLE]

    for r in range(slots // LANES):
        select = cols_select(v_esn[0:1, r * LANES : (r + 1) * LANES], nodes)
        p_node[:, r * LANES : (r + 1) * LANES] = select
    ready("nw0", "nw1", "nw2", "msn", "msnd", "mrcv", "me", "pw")
    own_rows = pl.ds(pl.multiple_of(band * share, 32), share)

    def fill_base():
        base_mid[...] = dot(v_mesh[own_rows, :], v_nw[0]) + v_bias[2, 0:1, :]

    def fill_send():
        for r in range(v_msn.shape[1] // LANES):
            column = down_column(v_msn[0:1, r * LANES : (r + 1) * LANES])
            g_send[r * LANES : (r + 1) * LANES, :] = rows_select(column, nodes)

    def fill_edges(part, parts):
        count = medges // LANES // parts

        @pl.loop(part * count, (part + 1) * count, unroll=2)
        def _(r):
            rows = pl.ds(pl.multiple_of(r * LANES, LANES), LANES)
            acc2[rows, :] = dot(v_me[rows, :], v_pw[0]) + v_bias[3, 0:1, :]
            g_msnd[rows, :] = rows_select(down_column(v_msnd[pl.ds(r, 1), :]), slots)

    fill_base()
    fill_send()

    def toward(c):
        return (left, right) if c == 0 else (right, left)

    def scatter_relay(c, far_copy, part, far, relay, relayed, sem_s, sem_r):
        first, _ = toward(c)
        far_copy.wait_recv()
        relay[c] = (far[c].astype(F32) + part[c, first].astype(F32)).astype(BF)
        copy = remote(relay.at[c], relayed.at[c], sem_s.at[c, 2], sem_r.at[c, 2], blk, first)
        copy.start()
        return copy

    pieces = []
    for c in range(NS):
        for copy in sum_copies[c]:
            copy.wait_recv()
        sums = dot(p_node[...], landed[c].reshape(slots, ws)).astype(BF)
        part[c] = sums.reshape(n_band, share, ws)
        copies = []
        for i, peer in enumerate((across, right, left)):
            copy = remote(part.at[c, peer], came.at[c, i], rs_s.at[c, i], rs_r.at[c, i], blk, peer)
            copy.start()
            copies.append(copy)
        pieces.append(copies)
        sent += copies

    first = base_mid[...]
    for c in range(NS):
        total = part[c, band].astype(F32)
        for i, copy in enumerate(pieces[c]):
            copy.wait_recv()
            total = total + came[c, i].astype(F32)
        first = first + dot(total.astype(BF), v_nw[1, c * ws : (c + 1) * ws, :])
    tail = norm(dot(silu(first).astype(BF), v_nw[2]) + v_bias[2, 1:2, :], v_gain[2:3, :])
    own_mid = (v_mesh[own_rows, :].astype(F32) + tail).astype(BF)
    mid[band] = own_mid

    gathers = {}

    def spread(m, hop):
        first_peer, other_peer = toward(m % 2)
        owner = other_peer if hop == 2 else band
        block = mid.at[owner, :, m * wm : (m + 1) * wm]
        gathers[m, hop] = remote(
            block, block, ag_s.at[m, hop], ag_r.at[m, hop], blk, other_peer if hop == 1 else first_peer
        )
        gathers[m, hop].start()

    def spread_own(half):
        for hop in range(2):
            for m in half:
                spread(m, hop)

    def spread_on(half):
        for m in half:
            gathers[m, 0].wait_recv()
            spread(m, 2)

    def pick(h, half):
        for m in half:
            gathers[m, 1].wait_recv()
            gathers[m, 2].wait_recv()
        picked = dot(g_send[...], mid[:, :, cols[h]].reshape(nodes, wc))
        srows[h] = picked.reshape(srows.shape[1:]).astype(BF)

    def to_everyone(h):
        @pl.loop(0, n_blk - 1)
        def _(i):
            step = (i + 1) // 2
            r = n_blk // 2 + step * (1 - 2 * lax.rem(i, 2))
            to = lax.rem(blk + r, n_blk)
            remote(srows.at[h, to], arr.at[h, blk], aa_s.at[h], aa_r.at[h], to, band).start()

        arr[h, blk] = srows[h, blk]

    halves = [range(h * NM // NC, (h + 1) * NM // NC) for h in range(NC)]
    spread_own(halves[0])
    spread_on(halves[0])
    spread_own(halves[1])
    pick(0, halves[0])
    spread_on(halves[1])
    to_everyone(0)
    pick(1, halves[1])
    to_everyone(1)
    fill_edges(0, 1)
    sent += list(gathers.values())

    tkeys[...] = dot(mid[...].reshape(nodes, width), v_pw[2]).astype(BF)

    @pl.loop(0, medges // LANES, unroll=2)
    def _(r):
        rows = pl.ds(pl.multiple_of(r * LANES, LANES), LANES)
        receiver_row = v_mrcv[pl.ds(r, 1), :]
        select = rows_select(down_column(receiver_row), nodes)
        acc2[rows, :] = acc2[rows, :] + dot(select, tkeys[...])
        r_rcv[:, rows] = cols_select(receiver_row, nodes)

    ready("gw")

    @pl.loop(0, v_grid.shape[0] // TILE, unroll=True)
    def _(t):
        rows = pl.ds(pl.multiple_of(t * TILE, TILE), TILE)
        first = dot(v_grid[rows, :], v_gw[0]) + v_bias[0, 0:1, :]
        tail = norm(dot(silu(first).astype(BF), v_gw[1]) + v_bias[0, 1:2, :], v_gain[0:1, :])
        v_go[rows, :] = (v_grid[rows, :].astype(F32) + tail).astype(BF)

    ready("fw")
    base_fin[...] = dot(mid[band], v_fw[0]) + v_bias[4, 0:1, :]

    blocks = pl.ds(0, n_blk - 1)
    everyone = [
        remote(srows.at[h, blocks], arr.at[h, blocks], aa_s.at[h], aa_r.at[h], blk, band)
        for h in range(NC)
    ]
    requested = None
    for h in range(NC):
        everyone[h].wait_recv()
        raw = arr[h].astype(F32).reshape(arr2.shape[0], wc).astype(BF)
        term = dot(raw, v_pw[1, cols[h], :])
        if h < NC - 1:
            opart[0 : arr2.shape[0], :] = term if requested is None else opart[0 : arr2.shape[0], :] + term
            requested = opart
        else:
            arr2[...] = (opart[0 : arr2.shape[0], :] + term).astype(BF)

    @pl.loop(0, medges // TILE, unroll=True)
    def _(t):
        rows = pl.ds(pl.multiple_of(t * TILE, TILE), TILE)
        first = acc2[rows, :] + dot(g_msnd[rows, :], arr2[...])
        second = dot(silu(first).astype(BF), v_pw[3]) + v_bias[3, 1:2, :]
        msg[rows, :] = norm(second, v_gain[3:4, :]).astype(BF)

    scatters = []
    for c in range(NC):
        def shared(peer):
            rows = pl.ds(pl.multiple_of(peer * share, 32), share)
            part2[c, peer] = dot(r_rcv[rows, :], msg[:, cols[c]]).astype(BF)

        shared(across)
        towards, other = toward(c)
        far_copy = remote(part2.at[c, across], far2.at[c], rt_s.at[c, 0], rt_r.at[c, 0], blk, towards)
        near_copy = remote(part2.at[c, other], near2.at[c], rt_s.at[c, 1], rt_r.at[c, 1], blk, other)
        far_copy.start()
        shared(other)
        shared(towards)
        shared(band)
        scatters.append((far_copy, near_copy))
    for far_copy, near_copy in scatters:
        far_copy.wait_send()
        near_copy.start()
    relays = []
    for c in range(NC):
        relays.append(scatter_relay(c, scatters[c][0], part2, far2, relay2, relayed2, rt_s, rt_r))
        sent += [scatters[c][1], relays[c]]
    first = base_fin[...]
    for c in range(NC):
        scatters[c][1].wait_recv()
        relays[c].wait_recv()
        total = part2[c, band].astype(F32) + near2[c].astype(F32) + relayed2[c].astype(F32)
        first = first + dot(total.astype(BF), v_fw[1, cols[c], :])
    tail = norm(dot(silu(first).astype(BF), v_fw[2]) + v_bias[4, 1:2, :], v_gain[4:5, :])
    for c in range(NC):
        v_mo[:, cols[c]] = (mid[band, :, cols[c]].astype(F32) + tail[:, cols[c]]).astype(BF)
    for copy in sent:
        copy.wait_send()
    for copy in everyone:
        copy.wait_send()


def handed_on(v_grid, v_mesh, grid_out, mesh_out, sem):
    copies = [
        pltpu.make_async_copy(v_mesh, mesh_out, sem.at[0]),
        pltpu.make_async_copy(v_grid, grid_out, sem.at[1]),
    ]
    for copy in copies:
        copy.start()
    for copy in copies:
        copy.wait()


def per_device(n_blk, n_band, *args):
    (grid_nodes, enc_edges, enc_sender, enc_slot, enc_slot_node, mesh_nodes, mesh_edges,
     mesh_sender, mesh_receiver, mesh_send_node, *params) = args

    def folded(index):
        return index.reshape(-1, LANES)

    args = (grid_nodes, enc_edges, folded(enc_sender), folded(enc_slot), enc_slot_node, mesh_nodes,
            mesh_edges, folded(mesh_sender), folded(mesh_receiver), mesh_send_node, *params)
    width = mesh_nodes.shape[1]
    wc = width // NC
    nodes = mesh_nodes.shape[0]
    share = nodes // n_band
    grid_rows = grid_nodes.shape[0]
    edges, medges = enc_edges.shape[0], mesh_edges.shape[0]
    slots = NEIGH * CAP
    requests = mesh_send_node.shape[1]
    vm = pltpu.VMEM
    dma = pltpu.SemaphoreType.DMA
    scratch = [vm(a.shape, a.dtype) for a in args]
    window = (NC, NEIGH, CAP, wc)
    shares, piece = (NC, n_band, share, wc), (NC, share, wc)
    boxes = (NC, n_blk, requests // n_blk, wc)
    ws = width // NS
    scratch += [vm(window, BF)] * 2 + [vm((NS, NEIGH, CAP, ws), BF)] * 2
    scratch += [vm((NS, n_band, share, ws), BF), vm((NS, n_band - 1, share, ws), BF)]
    scratch += [vm((n_band, share, width), BF), vm(boxes, BF), vm(boxes, BF), vm((requests, width), BF)]
    scratch += [vm(shares, BF)] + [vm(piece, BF)] * 4
    scratch += [
        vm((slots, nodes), BF), vm((edges, slots), BF), vm((slots, edges), BF),
        vm((edges, grid_rows), BF), vm((nodes, slots), BF), vm((requests, nodes), BF),
        vm((medges, requests), BF), vm((8, LANES), BF), vm((nodes, medges), BF),
    ]
    scratch += [
        vm((grid_rows, width), BF), vm((edges, width), F32), vm((medges, width), F32),
        vm((edges, width), F32), vm((max(edges, medges), width), BF), vm((share, width), F32),
        vm((share, width), F32), vm((slots, width), BF), vm((nodes, width), BF),
    ]
    near = len(WINDOWS)
    scratch += [dma((24,))]
    scratch += [dma((NC, near))] * 2 + [dma((NS, near))] * 2
    scratch += [dma((NS, 3))] * 2 + [dma((NM, 3))] * 2
    scratch += [dma((NC,))] * 2 + [dma((NC, 3))] * 2
    anywhere = pl.BlockSpec(memory_space=pl.ANY)
    on_chip = pl.BlockSpec(memory_space=pltpu.VMEM)
    results = pl.pallas_call(
        kernel,
        out_shape=(vm((grid_rows, width), BF), vm((share, width), BF)),
        in_specs=[anywhere] * len(args),
        out_specs=(on_chip, on_chip),
        scratch_shapes=scratch,
        compiler_params=pltpu.CompilerParams(
            collective_id=0, has_side_effects=True, vmem_limit_bytes=60 * 1024 * 1024
        ),
        name="encoder_processor",
    )(*args)
    return pl.pallas_call(
        handed_on,
        out_shape=tuple(jax.ShapeDtypeStruct(r.shape, r.dtype) for r in results),
        in_specs=[anywhere] * 2,
        out_specs=(anywhere, anywhere),
        scratch_shapes=[dma((2,))],
        name="handed_on",
    )(*[pltpu.with_memory_space_constraint(r, pltpu.VMEM) for r in results])


def solution(mesh):
    rows = P(("blk", "band"), None)
    flat = P(("blk", "band"))
    in_specs = (rows, rows, flat, flat, rows, P("blk", None), rows, flat, flat, rows) + (P(),) * 7
    n_blk, n_band = mesh.shape["blk"], mesh.shape["band"]

    def step(*args):
        return per_device(n_blk, n_band, *args)

    return jax.shard_map(
        step, mesh=mesh, in_specs=in_specs, out_specs=(rows, rows), check_vma=False
    )
```
